512 devices in a mesh: blk: 64 (over z, y_hi, core), split: 8 (over x, y_lo).
Axes of the slice: x: 4, y: 8 (y_hi: 4, y_lo: 2; y = y_hi * 2 + y_lo), z: 8, core: 2. Of those that a mesh axis runs over, the one named last changes fastest.
Arguments:
- user_factors: float32 [131072, 512], P(('blk', 'split')), may hold values from -2 to 2
- item_factors: float32 [8192, 512], P('blk'), may hold values from -2 to 2
- obs_items: int32 [131072, 4, 8], P(('blk', 'split')), may hold values from 0 to 127
- obs_conf: int32 [131072, 4, 8], P(('blk', 'split')), may hold values from 1 to 3
Outputs:
- users_out: float32 [131072, 512], P(('blk', 'split'))
- items_out: float32 [8192, 512], P(('blk', 'split'))
The draws below stay inside these ranges and needn't reach their ends.
All inputs are finite; a program needn't handle non-finite values.
Results may differ from the reference program's by a relative error of at most 0.0003.
Values sent between devices are 32-bit elements; how exact they have to be, the bound alone decides.
No kernel may reach another device: no remote copies, remote signals or barrier semaphores. Data moves between devices by JAX's collectives and lax.ppermute only.
A program may use at most 64 MiB of HBM per device.

```python
import jax
import jax.numpy as jnp
from jax import lax

R = 512
U_DEV = 256
I_SLAB = 128
OBS = 8
SUBS = 4
USERS = 131072
ITEMS = 8192
N_BLK = 64
N_SPLIT = 8


def touch_ends(drawn, rng, least, largest):
    index_at = [jax.random.randint(jax.random.fold_in(rng, axis), (), 0, length) for axis, length in enumerate(drawn.shape)]
    longest = drawn.shape.index(max(drawn.shape))
    neighbour = index_at[:longest] + [(index_at[longest] + 1) % drawn.shape[longest]] + index_at[longest + 1:]
    return drawn.at[tuple(index_at)].set(least).at[tuple(neighbour)].set(largest)


def steps_of(stream_key, extent, split, least, largest):
    loudness, own = 1.0, jax.random.fold_in(stream_key, 6)
    for axis_at, blocks in split:
        draws = jnp.exp(jax.random.uniform(jax.random.fold_in(own, axis_at), (blocks,), jnp.float32, least / len(split), largest / len(split)))
        loudness = loudness * jnp.repeat(draws, extent[axis_at] // blocks).reshape([-1 if axis == axis_at else 1 for axis in range(len(extent))])
    return loudness


def noise(stream_key, extent, width, bound, split=(), kind=jnp.bfloat16):
    values = width * jax.random.normal(stream_key, extent, jnp.float32)
    if split:
        values = values * steps_of(stream_key, extent, split, -0.22, 0.18)
    return jnp.clip(values, -bound, bound).astype(kind)


def setup_inputs(seed: int = 0) -> dict:
    streams_of = jax.random.split(jax.random.key(seed), 5)
    user_factors = noise(streams_of[0], (USERS, R), 0.25, 2.0, ((0, 512),), jnp.float32)
    item_factors = noise(streams_of[1], (ITEMS, R), 0.25, 2.0, ((0, 64),), jnp.float32)
    obs_items = touch_ends(jax.random.randint(streams_of[2], (USERS, SUBS, OBS), 0, I_SLAB), jax.random.fold_in(streams_of[2], 1), 0, I_SLAB - 1).astype(jnp.int32)
    obs_conf = touch_ends(jax.random.randint(streams_of[3], (USERS, SUBS, OBS), 1, 4), jax.random.fold_in(streams_of[3], 1), 1, 3).astype(jnp.int32)
    return {"user_factors": user_factors, "item_factors": item_factors, "obs_items": obs_items, "obs_conf": obs_conf}


LEARN_RATE = 0.0005
CONF_SCALE = 0.5
RIDGE_COEF = 0.01


def dense_counts(obs_rows, conf_rows, slab_rows):
    columns = lax.broadcasted_iota(jnp.int32, (1, 1, slab_rows), 2)
    hits = jnp.where(obs_rows[:, :, None] == columns, conf_rows[:, :, None].astype(jnp.float32), jnp.float32(0.0))
    return jnp.sum(hits, axis=1)


def block_step(user_rows, held, counts):
    scores = lax.dot_general(user_rows, held, (((1,), (1,)), ((), ())), precision=lax.Precision.HIGHEST, preferred_element_type=jnp.float32)
    target = jnp.where(counts > 0, 1.0, 0.0).astype(jnp.float32)
    weights = 1.0 + CONF_SCALE * counts
    errors = weights * (scores - target)
    grad_user = jnp.dot(errors, held, precision=lax.Precision.HIGHEST, preferred_element_type=jnp.float32) + RIDGE_COEF * user_rows
    partial_grad = lax.dot_general(errors, user_rows, (((0,), (0,)), ((), ())), precision=lax.Precision.HIGHEST, preferred_element_type=jnp.float32)
    return user_rows - LEARN_RATE * grad_user, partial_grad


def reference(user_factors, item_factors, obs_items, obs_conf):
    users_all = user_factors.reshape(N_BLK, U_DEV * N_SPLIT, R)
    held = item_factors.reshape(N_BLK, I_SLAB, R)
    items_all = obs_items.reshape(N_BLK, U_DEV * N_SPLIT, SUBS, OBS)
    conf_all = obs_conf.reshape(N_BLK, U_DEV * N_SPLIT, SUBS, OBS)

    def one_block(operands):
        user_rows, slab, obs_rows, conf_rows = operands
        counts = dense_counts(obs_rows, conf_rows, I_SLAB)
        new_rows, partial_grad = block_step(user_rows, slab, counts)
        return new_rows, slab - LEARN_RATE * (partial_grad + RIDGE_COEF * slab)

    for step in range(SUBS):
        users_all, held = lax.map(one_block, (users_all, held, items_all[:, :, step, :], conf_all[:, :, step, :]))
        held = jnp.roll(held, -1, axis=0)
    return users_all.reshape(USERS, R), held.reshape(ITEMS, R)
```

```python
import jax
import jax.numpy as jnp
from jax import lax
from jax.experimental import pallas as pl
from jax.experimental.pallas import tpu as pltpu
from jax.sharding import PartitionSpec as P

LEARN_RATE = 0.0005
CONF_SCALE = 0.5
RIDGE_COEF = 0.01
DECAY = 1.0 - LEARN_RATE * RIDGE_COEF
PARAMS = pltpu.CompilerParams(vmem_limit_bytes=8 << 20)

NT = (((1,), (1,)), ((), ()))
NN = (((1,), (0,)), ((), ()))
TN = (((0,), (0,)), ((), ()))


def halves(x):
    high = x.astype(jnp.bfloat16)
    low = (x - high.astype(jnp.float32)).astype(jnp.bfloat16)
    return high, low


def product(a, b, dims):
    def one(p, q):
        return lax.dot_general(p, q, dims, preferred_element_type=jnp.float32)

    return one(a[0], b[0]) + (one(a[0], b[1]) + one(a[1], b[0]))


def grad_kernel(user_ref, held_ref, items_ref, conf_ref, errors_ref, grad_ref):
    slab, users = errors_ref.shape
    rows = lax.broadcasted_iota(jnp.int32, (slab, users), 0)
    counts = jnp.zeros((slab, users), jnp.float32)
    for k in range(items_ref.shape[0]):
        hit = items_ref[k : k + 1, :] == rows
        counts += jnp.where(hit, conf_ref[k : k + 1, :].astype(jnp.float32), 0.0)
    user = halves(user_ref[...])
    scores = product(halves(held_ref[...]), user, NT)
    target = jnp.where(counts > 0.0, 1.0, 0.0)
    errors = (1.0 + CONF_SCALE * counts) * (scores - target)
    errors_ref[...] = errors
    grad_ref[...] = product(halves(errors), user, NN)


def gradient(user, held, items, conf):
    slab, users = held.shape[0], user.shape[0]
    return pl.pallas_call(
        grad_kernel,
        out_shape=(
            jax.ShapeDtypeStruct((slab, users), jnp.float32),
            jax.ShapeDtypeStruct(held.shape, jnp.float32),
        ),
        compiler_params=PARAMS,
        name="gradient",
    )(user, held, items, conf)


def user_kernel(user_ref, errors_ref, held_ref, out_ref):
    step = product(halves(errors_ref[...]), halves(held_ref[...]), TN)
    out_ref[...] = DECAY * user_ref[...] - LEARN_RATE * step


def update_users(user, errors, held):
    return pl.pallas_call(
        user_kernel,
        out_shape=jax.ShapeDtypeStruct(user.shape, jnp.float32),
        compiler_params=PARAMS,
        name="users",
    )(user, errors, held)


def share_kernel(parts_ref, share_ref, out_ref):
    total = parts_ref[0]
    for i in range(1, parts_ref.shape[0]):
        total += parts_ref[i]
    out_ref[...] = DECAY * share_ref[...] - LEARN_RATE * total


def update_share(parts, share):
    return pl.pallas_call(
        share_kernel,
        out_shape=jax.ShapeDtypeStruct(share.shape, jnp.float32),
        compiler_params=PARAMS,
        name="share",
    )(parts, share)


def local(user_factors, item_factors, obs_items, obs_conf):
    slab, rank = item_factors.shape
    n = lax.axis_size("split")
    blocks = lax.axis_size("blk")
    share_rows = slab // n
    back = [((b + 1) % blocks, b) for b in range(blocks)]
    user, held = user_factors, item_factors
    share = lax.dynamic_slice_in_dim(held, lax.axis_index("split") * share_rows, share_rows, 0)
    items = jnp.transpose(obs_items, (1, 2, 0))
    conf = jnp.transpose(obs_conf, (1, 2, 0))
    steps = items.shape[0]
    for step in range(steps):
        errors, grad = gradient(user, held, items[step], conf[step])
        parts = lax.all_to_all(grad.reshape(n, share_rows, rank), "split", 0, 0)
        share = lax.ppermute(update_share(parts, share), "blk", back)
        user = update_users(user, errors, held)
        if step < steps - 1:
            copies = jnp.broadcast_to(share[None], (n, share_rows, rank))
            held = lax.all_to_all(copies, "split", 0, 0).reshape(slab, rank)
    return user, share


def solution(mesh):
    in_specs = (
        P(("blk", "split"), None),
        P("blk", None),
        P(("blk", "split"), None, None),
        P(("blk", "split"), None, None),
    )
    out_specs = (P(("blk", "split"), None), P(("blk", "split"), None))
    return jax.shard_map(local, mesh=mesh, in_specs=in_specs, out_specs=out_specs, check_vma=False)
```

```python
import functools

import jax
import jax.numpy as jnp
from jax import lax
from jax.experimental import pallas as pl
from jax.experimental.pallas import tpu as pltpu
from jax.sharding import PartitionSpec as P

LEARN_RATE = 0.0005
CONF_SCALE = 0.5
RIDGE_COEF = 0.01
DECAY = 1.0 - LEARN_RATE * RIDGE_COEF
PARAMS = pltpu.CompilerParams(vmem_limit_bytes=16 << 20)

NT = (((1,), (1,)), ((), ()))
NN = (((1,), (0,)), ((), ()))
TN = (((0,), (0,)), ((), ()))

MATES = (1, 2, 3)
MIRROR = 6


def halves(x):
    high = x.astype(jnp.bfloat16)
    low = (x - high.astype(jnp.float32)).astype(jnp.bfloat16)
    return high, low


def product(a, b, dims):
    def one(p, q):
        return lax.dot_general(p, q, dims, preferred_element_type=jnp.float32)

    return one(a[0], b[0]) + (one(a[0], b[1]) + one(a[1], b[0]))


def errors_of(held, user, items, conf, rows):
    counts = jnp.zeros(rows.shape, jnp.float32)
    for k in range(items.shape[0]):
        counts += jnp.where(items[k : k + 1] == rows, conf[k : k + 1], 0.0)
    target = jnp.where(counts > 0.0, 1.0, 0.0)
    return (1.0 + CONF_SCALE * counts) * (product(held, user, NT) - target)


def iota_rows(slab, users):
    return lax.broadcasted_iota(jnp.int32, (slab, users), 0)


def packed(ref, users, step, obs):
    at = users + (step - 1) * obs
    items = ref[at : at + obs, :users].astype(jnp.int32)
    return items, ref[at : at + obs, users:]


def call(kernel, outs, name):
    return pl.pallas_call(
        kernel,
        out_shape=[jax.ShapeDtypeStruct(o, jnp.float32) for o in outs],
        compiler_params=PARAMS,
        name=name,
    )


def first_kernel(user_ref, held_ref, items_ref, conf_ref, errors_ref, grad_ref):
    user = halves(user_ref[...])
    rows = iota_rows(*errors_ref.shape)
    conf = conf_ref[0].astype(jnp.float32)
    errors = errors_of(halves(held_ref[...]), user, items_ref[0], conf, rows)
    errors_ref[...] = errors
    grad_ref[...] = product(halves(errors), user, NN)


def pack_kernel(user_ref, held_ref, errors_ref, items_ref, conf_ref, out_ref):
    users = user_ref.shape[0]
    steps, obs, _ = items_ref.shape
    step = product(halves(errors_ref[...]), halves(held_ref[...]), TN)
    out_ref[:users, :] = DECAY * user_ref[...] - LEARN_RATE * step
    for s in range(1, steps):
        at = users + (s - 1) * obs
        out_ref[at : at + obs, :users] = items_ref[s].astype(jnp.float32)
        out_ref[at : at + obs, users:] = conf_ref[s].astype(jnp.float32)


def share_kernel(parts_ref, held_ref, out_ref):
    share = out_ref.shape[0]
    total = parts_ref[0]
    for i in range(1, parts_ref.shape[0]):
        total += parts_ref[i]
    at = pl.multiple_of(lax.axis_index("split") * share, share)
    out_ref[...] = DECAY * held_ref[pl.ds(at, share), :] - LEARN_RATE * total


def copies_kernel(share_ref, out_ref):
    for i in range(out_ref.shape[0]):
        out_ref[i] = share_ref[...]


def slab_of(refs):
    held = refs[0][...]
    for ref in refs[1:]:
        held += ref[...]
    return held


def group_kernel(step, obs, pieces, *refs):
    n = len(MATES) + 1
    held_refs, user_refs, pack_refs = refs[:pieces], refs[pieces : pieces + n], refs[pieces + n : pieces + 2 * n]
    errors_ref, same_ref, mirror_ref = refs[pieces + 2 * n :]
    _, slab, users = errors_ref.shape
    held = slab_of(held_refs)
    held_halves = halves(held)
    rows = iota_rows(slab, users)
    total = jnp.zeros(held.shape, jnp.float32)
    for i in range(n):
        user = halves(user_refs[i][:users, :])
        items, conf = packed(pack_refs[i], users, step, obs)
        errors = errors_of(held_halves, user, items, conf, rows)
        errors_ref[i] = errors
        total += product(halves(errors), user, NN)
    mirror = -LEARN_RATE * total
    mirror_ref[...] = mirror
    same_ref[...] = DECAY * held + mirror


def group_users_kernel(pieces, *refs):
    n = len(MATES) + 1
    held_refs, errors_ref, user_refs, out_refs = refs[:pieces], refs[pieces], refs[pieces + 1 : pieces + 1 + n], refs[pieces + 1 + n :]
    held = halves(slab_of(held_refs))
    users = out_refs[0].shape[0]
    for i in range(n):
        step = product(halves(errors_ref[i]), held, TN)
        out_refs[i][...] = DECAY * user_refs[i][:users, :] - LEARN_RATE * step


def last_kernel(step, obs, same_ref, mirror_ref, *refs):
    n = len(MATES) + 1
    user_refs, pack_refs = refs[:n], refs[n : 2 * n]
    out_same_ref, out_mirror_ref = refs[2 * n :]
    share = out_same_ref.shape[0]
    users = user_refs[0].shape[0]
    place = lax.axis_index("split")
    at = [pl.multiple_of(place * share, share), pl.multiple_of((place ^ MIRROR) * share, share)]
    pieces = [same_ref[pl.ds(a, share), :] + mirror_ref[pl.ds(a, share), :] for a in at]
    held = halves(jnp.concatenate(pieces, axis=0))
    inner = iota_rows(2 * share, users)
    rows = jnp.where(inner < share, inner + at[0], inner + (at[1] - share))
    total = jnp.zeros((2 * share, same_ref.shape[1]), jnp.float32)
    for i in range(n):
        user = halves(user_refs[i][...])
        items, conf = packed(pack_refs[i], users, step, obs)
        errors = errors_of(held, user, items, conf, rows)
        total += product(halves(errors), user, NN)
    out_same_ref[...] = DECAY * pieces[0] - LEARN_RATE * total[:share]
    out_mirror_ref[...] = -LEARN_RATE * total[share:]


def sum_kernel(a_ref, b_ref, out_ref):
    out_ref[...] = a_ref[...] + b_ref[...]


def last_users_kernel(step, obs, same_ref, mirror_ref, user_ref, pack_ref, out_ref):
    users = user_ref.shape[0]
    held = halves(same_ref[...] + mirror_ref[...])
    user = user_ref[...]
    items, conf = packed(pack_ref, users, step, obs)
    errors = errors_of(held, halves(user), items, conf, iota_rows(same_ref.shape[0], users))
    out_ref[...] = DECAY * user - LEARN_RATE * product(halves(errors), held, TN)


def local(user_factors, item_factors, obs_items, obs_conf):
    slab, rank = item_factors.shape
    users = user_factors.shape[0]
    _, steps, obs = obs_items.shape
    n = lax.axis_size("split")
    blocks = lax.axis_size("blk")
    share_rows = slab // n
    back = [((b + 1) % blocks, b) for b in range(blocks)]
    back_mirror = [(((b + 1) % blocks) * n + (k ^ MIRROR), b * n + k) for b in range(blocks) for k in range(n)]
    items = jnp.transpose(obs_items, (1, 2, 0))
    conf = jnp.transpose(obs_conf, (1, 2, 0))

    def onward(same, mirror):
        return [lax.ppermute(same, "blk", back), lax.ppermute(mirror, ("blk", "split"), back_mirror)]

    errors, grad = call(first_kernel, [(slab, users), (slab, rank)], "first")(user_factors, item_factors, items, conf)
    parts = lax.all_to_all(grad.reshape(n, share_rows, rank), "split", 0, 0)
    rows = users + (steps - 1) * obs
    (own,) = call(pack_kernel, [(rows, rank)], "pack")(user_factors, item_factors, errors, items, conf)
    packs = [own] + [lax.ppermute(own, "split", [(k, k ^ m) for k in range(n)]) for m in MATES]
    (share,) = call(share_kernel, [(share_rows, rank)], "share")(parts, item_factors)
    share = lax.ppermute(share, "blk", back)
    (copies,) = call(copies_kernel, [(n, share_rows, rank)], "copies")(share)
    held = [lax.all_to_all(copies, "split", 0, 0).reshape(slab, rank)]

    user = packs
    for step in range(1, steps - 1):
        kernel = functools.partial(group_kernel, step, obs, len(held))
        outs = [(len(packs), slab, users), (slab, rank), (slab, rank)]
        errors, same, mirror = call(kernel, outs, "group")(*held, *user, *packs)
        sent = onward(same, mirror)
        kernel = functools.partial(group_users_kernel, len(held))
        user = call(kernel, [(users, rank)] * len(packs), "group_users")(*held, errors, *user)
        held = sent
    kernel = functools.partial(last_kernel, steps - 1, obs)
    same, mirror = call(kernel, [(share_rows, rank)] * 2, "last")(*held, *user, *packs)
    same, mirror = onward(same, mirror)
    kernel = functools.partial(last_users_kernel, steps - 1, obs)
    (user_out,) = call(kernel, [(users, rank)], "last_users")(*held, user[0], packs[0])
    (share_out,) = call(sum_kernel, [(share_rows, rank)], "total")(same, mirror)
    return user_out, share_out


def solution(mesh):
    in_specs = (
        P(("blk", "split"), None),
        P("blk", None),
        P(("blk", "split"), None, None),
        P(("blk", "split"), None, None),
    )
    out_specs = (P(("blk", "split"), None), P(("blk", "split"), None))
    return jax.shard_map(local, mesh=mesh, in_specs=in_specs, out_specs=out_specs, check_vma=False)
```

```python
import functools

import jax
import jax.numpy as jnp
from jax import lax
from jax.experimental import pallas as pl
from jax.experimental.pallas import tpu as pltpu
from jax.sharding import PartitionSpec as P

LEARN_RATE = 0.0005
CONF_SCALE = 0.5
RIDGE_COEF = 0.01
DECAY = 1.0 - LEARN_RATE * RIDGE_COEF
PARAMS = pltpu.CompilerParams(vmem_limit_bytes=16 << 20)

NT = (((1,), (1,)), ((), ()))
NN = (((1,), (0,)), ((), ()))
TN = (((0,), (0,)), ((), ()))

FIRST, SECOND = 2, 7
HELPERS = ((0, 5), (4, 1), (3, 6))


def halves(x):
    high = x.astype(jnp.bfloat16)
    low = (x - high.astype(jnp.float32)).astype(jnp.bfloat16)
    return high, low


def product(a, b, dims):
    def one(p, q):
        return lax.dot_general(p, q, dims, preferred_element_type=jnp.float32)

    return one(a[0], b[0]) + (one(a[0], b[1]) + one(a[1], b[0]))


def errors_of(held, user, items, conf):
    rows = lax.broadcasted_iota(jnp.int32, (held[0].shape[0], user[0].shape[0]), 0)
    counts = jnp.zeros(rows.shape, jnp.float32)
    for k in range(items.shape[0]):
        counts += jnp.where(items[k : k + 1] == rows, conf[k : k + 1], 0.0)
    target = jnp.where(counts > 0.0, 1.0, 0.0)
    return (1.0 + CONF_SCALE * counts) * (product(held, user, NT) - target)


def packed(ref, users, step, obs):
    at = users + step * obs
    return ref[at : at + obs, :users].astype(jnp.int32), ref[at : at + obs, users:]


def parity():
    return lax.axis_index("blk") & 1


def slab_of(refs):
    held = refs[0][...]
    for ref in refs[1:]:
        held += ref[...]
    return held


def call(kernel, outs, name, params=PARAMS, **kwargs):
    return pl.pallas_call(
        kernel,
        out_shape=[jax.ShapeDtypeStruct(o, jnp.float32) for o in outs],
        compiler_params=params,
        name=name,
        **kwargs,
    )


def pack_kernel(user_ref, held_ref, items_ref, conf_ref, out_ref, slab_ref, items, conf, sems):
    users = user_ref.shape[0]
    steps, obs, _ = items_ref.shape
    copies = [
        pltpu.make_async_copy(items_ref, items, sems.at[0]),
        pltpu.make_async_copy(conf_ref, conf, sems.at[1]),
        pltpu.make_async_copy(user_ref, out_ref.at[pl.ds(0, users), :], sems.at[2]),
        pltpu.make_async_copy(held_ref, slab_ref, sems.at[3]),
    ]
    for copy in copies:
        copy.start()
    copies[0].wait()
    copies[1].wait()
    for s in range(steps):
        at = users + s * obs
        out_ref[at : at + obs, :users] = items[s].astype(jnp.float32)
        out_ref[at : at + obs, users:] = conf[s].astype(jnp.float32)
    copies[2].wait()
    copies[3].wait()


def group_kernel(step, obs, pieces, chunks, *refs):
    held_refs, refs = refs[:pieces], refs[pieces:]
    user_refs, pack_refs, (errors_ref, out_ref) = refs[:chunks], refs[chunks : 2 * chunks], refs[2 * chunks :]
    _, slab, users = errors_ref.shape
    held = slab_of(held_refs)
    held_halves = halves(held)
    total = jnp.zeros(held.shape, jnp.float32)
    for i in range(chunks):
        user = halves(user_refs[i][:users, :])
        errors = errors_of(held_halves, user, *packed(pack_refs[i], users, step, obs))
        errors_ref[i] = errors
        total += product(halves(errors), user, NN)
    keep = jnp.where((lax.axis_index("split") ^ parity()) == FIRST, DECAY, 0.0)
    out_ref[...] = keep * held - LEARN_RATE * total


def users_kernel(pieces, chunks, *refs):
    held_refs, errors_ref, refs = refs[:pieces], refs[pieces], refs[pieces + 1 :]
    user_refs, out_refs = refs[:chunks], refs[chunks:]
    held = halves(slab_of(held_refs))
    users = out_refs[0].shape[0]
    for i in range(chunks):
        step = product(halves(errors_ref[i]), held, TN)
        out_refs[i][...] = DECAY * user_refs[i][:users, :] - LEARN_RATE * step


def share_kernel(parts_ref, out_ref):
    out_ref[...] = parts_ref[FIRST ^ parity()] + parts_ref[SECOND ^ parity()]


def home_kernel(share_ref, own_ref, a_ref, b_ref, c_ref, out_ref, share_out_ref):
    share_out_ref[...] = share_ref[...]
    place = lax.axis_index("split") ^ parity()
    works = (place == FIRST) | (place == SECOND)

    @pl.when(works)
    def _():
        out_ref[...] = own_ref[...]

    @pl.when(jnp.logical_not(works))
    def _():
        out_ref[...] = a_ref[...] + b_ref[...] + c_ref[...]


def local(user_factors, item_factors, obs_items, obs_conf):
    slab, rank = item_factors.shape
    users = user_factors.shape[0]
    _, steps, obs = obs_items.shape
    n = lax.axis_size("split")
    blocks = lax.axis_size("blk")
    share_rows = slab // n
    chunks = 1 + len(HELPERS)
    items = jnp.transpose(obs_items, (1, 2, 0))
    conf = jnp.transpose(obs_conf, (1, 2, 0))
    both = ("blk", "split")

    def at(b, k):
        return b * n + (k ^ (b & 1))

    def fetch(x, helpers):
        pairs = [(at(b, h), at(b, w)) for b in range(blocks) for h, w in zip(helpers, (FIRST, SECOND))]
        return lax.ppermute(x, both, pairs)

    def give(x, helpers):
        pairs = [(at(b, w), at(b, h)) for b in range(blocks) for h, w in zip(helpers, (FIRST, SECOND))]
        return lax.ppermute(x, both, pairs)

    def onward(x):
        same, cross = [], []
        for b in range(blocks):
            for w, v in ((FIRST, SECOND), (SECOND, FIRST)):
                source = at((b + 1) % blocks, w)
                same.append((source, at(b, w)))
                cross.append((source, at(b, v)))
        return [lax.ppermute(x, both, same), lax.ppermute(x, both, cross)]

    hbm = pl.BlockSpec(memory_space=pltpu.HBM)
    own, held = call(
        pack_kernel,
        [(users + steps * obs, rank), (slab, rank)],
        "pack",
        params=None,
        in_specs=[hbm] * 4,
        scratch_shapes=[pltpu.VMEM(items.shape, jnp.int32)] * 2 + [pltpu.SemaphoreType.DMA((4,))],
    )(user_factors, item_factors, items, conf)
    packs = [own] + [fetch(own, helpers) for helpers in HELPERS]
    user, held = packs, [held]
    for step in range(steps):
        kernel = functools.partial(group_kernel, step, obs, len(held), chunks)
        errors, out = call(kernel, [(chunks, slab, users), (slab, rank)], "group")(*held, *user, *packs)
        if step < steps - 1:
            sent = onward(out)
        else:
            parts = lax.all_to_all(out.reshape(n, share_rows, rank), "split", 0, 0)
        kernel = functools.partial(users_kernel, len(held), chunks)
        user = call(kernel, [(users, rank)] * chunks, "users")(*held, errors, *user)
        held = sent
    early = pl.CostEstimate(flops=1 << 36, bytes_accessed=1 << 20, transcendentals=0)
    (share,) = call(share_kernel, [(share_rows, rank)], "share", cost_estimate=early)(parts)
    share = lax.ppermute(share, "blk", [((b + 1) % blocks, b) for b in range(blocks)])
    home = [give(u, helpers) for u, helpers in zip(user[1:], HELPERS)]
    outs = [(users, rank), (share_rows, rank)]
    user_out, share_out = call(home_kernel, outs, "home")(share, user[0], *home)
    return user_out, share_out


def solution(mesh):
    in_specs = (
        P(("blk", "split"), None),
        P("blk", None),
        P(("blk", "split"), None, None),
        P(("blk", "split"), None, None),
    )
    out_specs = (P(("blk", "split"), None), P(("blk", "split"), None))
    return jax.shard_map(local, mesh=mesh, in_specs=in_specs, out_specs=out_specs, check_vma=False)
```

```python
import functools

import jax
import jax.numpy as jnp
from jax import lax
from jax.experimental import pallas as pl
from jax.experimental.pallas import tpu as pltpu
from jax.sharding import PartitionSpec as P

LEARN_RATE = 0.0005
CONF_SCALE = 0.5
RIDGE_COEF = 0.01
DECAY = 1.0 - LEARN_RATE * RIDGE_COEF
PARAMS = pltpu.CompilerParams(vmem_limit_bytes=16 << 20)

NT = (((1,), (1,)), ((), ()))
NN = (((1,), (0,)), ((), ()))
TN = (((0,), (0,)), ((), ()))

FIRST, SECOND = 2, 7
HELPERS = ((0, 5), (4, 1), (3, 6))


def halves(x):
    high = x.astype(jnp.bfloat16)
    low = (x - high.astype(jnp.float32)).astype(jnp.bfloat16)
    return high, low


def product(a, b, dims):
    def one(p, q):
        return lax.dot_general(p, q, dims, preferred_element_type=jnp.float32)

    return one(a[0], b[0]) + (one(a[0], b[1]) + one(a[1], b[0]))


def errors_of(held, user, items, conf):
    rows = lax.broadcasted_iota(jnp.int32, (held[0].shape[0], user[0].shape[0]), 0)
    counts = jnp.zeros(rows.shape, jnp.float32)
    for k in range(items.shape[0]):
        counts += jnp.where(items[k : k + 1] == rows, conf[k : k + 1], 0.0)
    target = jnp.where(counts > 0.0, 1.0, 0.0)
    return (1.0 + CONF_SCALE * counts) * (product(held, user, NT) - target)


def listed(ref, users, step, obs):
    at = users + step * obs
    return ref[at : at + obs, :users].astype(jnp.int32), ref[at : at + obs, users:]


def parity():
    return lax.axis_index("blk") & 1


def slab_of(refs):
    held = refs[0][...]
    for ref in refs[1:]:
        held += ref[...]
    return held


def call(kernel, outs, name, params=PARAMS, **kwargs):
    return pl.pallas_call(
        kernel,
        out_shape=[jax.ShapeDtypeStruct(o, jnp.float32) for o in outs],
        compiler_params=params,
        name=name,
        **kwargs,
    )


def pack_kernel(user_ref, items_ref, conf_ref, out_ref, items, conf, lists, sems):
    users = user_ref.shape[0]
    steps, obs, _ = items_ref.shape
    body = pltpu.make_async_copy(user_ref, out_ref.at[pl.ds(0, users), :], sems.at[0])
    loads = [
        pltpu.make_async_copy(items_ref, items, sems.at[1]),
        pltpu.make_async_copy(conf_ref, conf, sems.at[2]),
    ]
    for copy in (*loads, body):
        copy.start()
    for copy in loads:
        copy.wait()
    for s in range(steps):
        at = s * obs
        lists[at : at + obs, :users] = items[s].astype(jnp.float32)
        lists[at : at + obs, users:] = conf[s].astype(jnp.float32)
    tail = pltpu.make_async_copy(lists, out_ref.at[pl.ds(users, steps * obs), :], sems.at[3])
    tail.start()
    tail.wait()
    body.wait()


def kept():
    return jnp.where((lax.axis_index("split") ^ parity()) == FIRST, DECAY, 0.0)


def own_kernel(step, obs, held_ref, user_ref, errors_ref, total_ref):
    users = errors_ref.shape[1]
    user = halves(user_ref[:users, :])
    errors = errors_of(halves(held_ref[...]), user, *listed(user_ref, users, step, obs))
    errors_ref[...] = errors
    total_ref[...] = product(halves(errors), user, NN)


def group_kernel(step, obs, pieces, totals, chunks, *refs):
    held_refs, total_refs, refs = refs[:pieces], refs[pieces : pieces + totals], refs[pieces + totals :]
    user_refs, list_refs, out_ref, errors_refs = refs[:chunks], refs[chunks : 2 * chunks], refs[2 * chunks], refs[2 * chunks + 1 :]
    held = slab_of(held_refs)
    held_halves = halves(held)
    total = total_refs[0][...] if totals else jnp.zeros(held.shape, jnp.float32)
    for user_ref, list_ref, errors_ref in zip(user_refs, list_refs, errors_refs):
        users = errors_ref.shape[1]
        user = halves(user_ref[:users, :])
        errors = errors_of(held_halves, user, *listed(list_ref, users, step, obs))
        errors_ref[...] = errors
        total += product(halves(errors), user, NN)
    out_ref[...] = kept() * held - LEARN_RATE * total


def users_kernel(pieces, chunks, *refs):
    held_refs, errors_refs, refs = refs[:pieces], refs[pieces : pieces + chunks], refs[pieces + chunks :]
    user_refs, out_refs = refs[:chunks], refs[chunks:]
    held = halves(slab_of(held_refs))
    for errors_ref, user_ref, out_ref in zip(errors_refs, user_refs, out_refs):
        step = product(halves(errors_ref[...]), held, TN)
        out_ref[...] = DECAY * user_ref[: out_ref.shape[0], :] - LEARN_RATE * step


def last_kernel(step, obs, pieces, chunks, *refs):
    held_refs, refs = refs[:pieces], refs[pieces:]
    user_refs, list_refs, out_ref, new_refs = refs[:chunks], refs[chunks : 2 * chunks], refs[2 * chunks], refs[2 * chunks + 1 :]
    held = slab_of(held_refs)
    held_halves = halves(held)
    total = jnp.zeros(held.shape, jnp.float32)
    for user_ref, list_ref, new_ref in zip(user_refs, list_refs, new_refs):
        user = user_ref[...]
        user_halves = halves(user)
        errors = errors_of(held_halves, user_halves, *listed(list_ref, user_ref.shape[0], step, obs))
        errors = halves(errors)
        total += product(errors, user_halves, NN)
        new_ref[...] = DECAY * user - LEARN_RATE * product(errors, held_halves, TN)
    out_ref[...] = kept() * held - LEARN_RATE * total


def share_kernel(parts_ref, out_ref):
    out_ref[...] = parts_ref[FIRST ^ parity()] + parts_ref[SECOND ^ parity()]


def home_kernel(share_ref, own_ref, a_ref, b_ref, c_ref, out_ref, share_out_ref, sem):
    share_out_ref[...] = share_ref[...]
    place = lax.axis_index("split") ^ parity()
    for ref, places in zip((own_ref, a_ref, b_ref, c_ref), ((FIRST, SECOND), *HELPERS)):

        @pl.when((place == places[0]) | (place == places[1]))
        def _(ref=ref):
            copy = pltpu.make_async_copy(ref, out_ref, sem)
            copy.start()
            copy.wait()


def local(user_factors, item_factors, obs_items, obs_conf):
    slab, rank = item_factors.shape
    users = user_factors.shape[0]
    _, steps, obs = obs_items.shape
    n = lax.axis_size("split")
    blocks = lax.axis_size("blk")
    share_rows = slab // n
    chunks = 1 + len(HELPERS)
    items = jnp.transpose(obs_items, (1, 2, 0))
    conf = jnp.transpose(obs_conf, (1, 2, 0))
    both = ("blk", "split")

    def at(b, k):
        return b * n + (k ^ (b & 1))

    def fetch(x, helpers):
        pairs = [(at(b, h), at(b, w)) for b in range(blocks) for h, w in zip(helpers, (FIRST, SECOND))]
        return lax.ppermute(x, both, pairs)

    def give(x, helpers):
        pairs = [(at(b, w), at(b, h)) for b in range(blocks) for h, w in zip(helpers, (FIRST, SECOND))]
        return lax.ppermute(x, both, pairs)

    def onward(x):
        same, cross = [], []
        for b in range(blocks):
            for w, v in ((FIRST, SECOND), (SECOND, FIRST)):
                source = at((b + 1) % blocks, w)
                same.append((source, at(b, w)))
                cross.append((source, at(b, v)))
        return [lax.ppermute(x, both, same), lax.ppermute(x, both, cross)]

    hbm = pl.BlockSpec(memory_space=pltpu.HBM)
    lists_rows = steps * obs
    (own,) = call(
        pack_kernel,
        [(users + lists_rows, rank)],
        "pack",
        params=None,
        in_specs=[hbm] * 3,
        out_specs=[hbm],
        scratch_shapes=[pltpu.VMEM(items.shape, jnp.int32)] * 2
        + [pltpu.VMEM((lists_rows, rank), jnp.float32), pltpu.SemaphoreType.DMA((4,))],
    )(user_factors, items, conf)
    packs = [own] + [fetch(own, helpers) for helpers in HELPERS]
    user = packs
    held = [item_factors]
    for step in range(steps - 1):
        if step == 0:
            kernel = functools.partial(own_kernel, step, obs)
            own_errors, total = call(kernel, [(slab, users), (slab, rank)], "own")(item_factors, own)
            first, totals = [own_errors], [total]
        else:
            first, totals = [], []
        rest = chunks - len(first)
        kernel = functools.partial(group_kernel, step, obs, len(held), len(totals), rest)
        outs = [(slab, rank)] + [(slab, users)] * rest
        out, *errors = call(kernel, outs, "group")(*held, *totals, *user[-rest:], *packs[-rest:])
        sent = onward(out)
        kernel = functools.partial(users_kernel, len(held), chunks)
        user = call(kernel, [(users, rank)] * chunks, "users")(*held, *first, *errors, *user)
        held = sent
    kernel = functools.partial(last_kernel, steps - 1, obs, len(held), chunks)
    out, *user = call(kernel, [(slab, rank)] + [(users, rank)] * chunks, "last")(*held, *user, *packs)
    parts = lax.all_to_all(out.reshape(n, share_rows, rank), "split", 0, 0)
    early = pl.CostEstimate(flops=1 << 36, bytes_accessed=1 << 20, transcendentals=0)
    (share,) = call(share_kernel, [(share_rows, rank)], "share", cost_estimate=early)(parts)
    share = lax.ppermute(share, "blk", [((b + 1) % blocks, b) for b in range(blocks)])
    home = [give(u, helpers) for u, helpers in zip(user[1:], HELPERS)]
    user_out, share_out = call(
        home_kernel,
        [(users, rank), (share_rows, rank)],
        "home",
        out_specs=[pl.BlockSpec(memory_space=pltpu.HBM), pl.BlockSpec(memory_space=pltpu.VMEM)],
        scratch_shapes=[pltpu.SemaphoreType.DMA],
    )(share, user[0], *home)
    return user_out, share_out


def solution(mesh):
    in_specs = (
        P(("blk", "split"), None),
        P("blk", None),
        P(("blk", "split"), None, None),
        P(("blk", "split"), None, None),
    )
    out_specs = (P(("blk", "split"), None), P(("blk", "split"), None))
    return jax.shard_map(local, mesh=mesh, in_specs=in_specs, out_specs=out_specs, check_vma=False)
```

```python
import functools

import jax
import jax.numpy as jnp
from jax import lax
from jax.experimental import pallas as pl
from jax.experimental.pallas import tpu as pltpu
from jax.sharding import PartitionSpec as P

LEARN_RATE = 0.0005
CONF_SCALE = 0.5
RIDGE_COEF = 0.01
DECAY = 1.0 - LEARN_RATE * RIDGE_COEF
PARAMS = pltpu.CompilerParams(vmem_limit_bytes=16 << 20)

NT = (((1,), (1,)), ((), ()))
NN = (((1,), (0,)), ((), ()))
TN = (((0,), (0,)), ((), ()))

FIRST, SECOND = 2, 7
PIECES = 4
HELPERS = ((0, 5), (4, 1), (3, 6))


def halves(x):
    high = x.astype(jnp.bfloat16)
    low = (x - high.astype(jnp.float32)).astype(jnp.bfloat16)
    return high, low


def product(a, b, dims):
    def one(p, q):
        return lax.dot_general(p, q, dims, preferred_element_type=jnp.float32)

    return one(a[0], b[0]) + (one(a[0], b[1]) + one(a[1], b[0]))


def errors_of(held, user, items, conf):
    rows = lax.broadcasted_iota(jnp.int32, (held[0].shape[0], user[0].shape[0]), 0)
    counts = jnp.zeros(rows.shape, jnp.float32)
    for k in range(items.shape[0]):
        counts += jnp.where(items[k : k + 1] == rows, conf[k : k + 1], 0.0)
    target = jnp.where(counts > 0.0, 1.0, 0.0)
    return (1.0 + CONF_SCALE * counts) * (product(held, user, NT) - target)


def listed(ref, users, step, obs):
    at = users + step * obs
    return ref[at : at + obs, :users].astype(jnp.int32), ref[at : at + obs, users:]


def parity():
    return lax.axis_index("blk") & 1


def slab_of(refs):
    held = refs[0][...]
    for ref in refs[1:]:
        held += ref[...]
    return held


def call(kernel, outs, name, params=PARAMS, **kwargs):
    return pl.pallas_call(
        kernel,
        out_shape=[jax.ShapeDtypeStruct(o, jnp.float32) for o in outs],
        compiler_params=params,
        name=name,
        **kwargs,
    )


def pack_kernel(user_ref, items_ref, conf_ref, out_ref, items, conf, pack, load_sems, store_sems):
    users = user_ref.shape[0]
    steps, obs, _ = items_ref.shape
    rows = steps * obs
    pieces = load_sems.shape[0] - 2
    size = users // pieces
    loads = [
        pltpu.make_async_copy(items_ref, items, load_sems.at[pieces]),
        pltpu.make_async_copy(conf_ref, conf, load_sems.at[pieces + 1]),
    ]
    places = [pl.ds(i * size, size) for i in range(pieces)]
    bodies = [pltpu.make_async_copy(user_ref.at[p, :], pack.at[p, :], load_sems.at[i]) for i, p in enumerate(places)]
    places.append(pl.ds(users, rows))
    stores = [pltpu.make_async_copy(pack.at[p, :], out_ref.at[p, :], store_sems.at[i]) for i, p in enumerate(places)]
    for copy in (*loads, *bodies):
        copy.start()
    for copy in loads:
        copy.wait()
    for s in range(steps):
        at = users + s * obs
        pack[at : at + obs, :users] = items[s].astype(jnp.float32)
        pack[at : at + obs, users:] = conf[s].astype(jnp.float32)
    stores[pieces].start()
    for i in range(pieces):
        bodies[i].wait()
        stores[i].start()
    for copy in stores:
        copy.wait()


def kept():
    return jnp.where((lax.axis_index("split") ^ parity()) == FIRST, DECAY, 0.0)


def own_kernel(step, obs, held_ref, user_ref, errors_ref, total_ref):
    users = errors_ref.shape[1]
    user = halves(user_ref[:users, :])
    errors = errors_of(halves(held_ref[...]), user, *listed(user_ref, users, step, obs))
    errors_ref[...] = errors
    total_ref[...] = product(halves(errors), user, NN)


def group_kernel(step, obs, pieces, totals, chunks, *refs):
    held_refs, total_refs, refs = refs[:pieces], refs[pieces : pieces + totals], refs[pieces + totals :]
    user_refs, list_refs, out_ref, errors_refs = refs[:chunks], refs[chunks : 2 * chunks], refs[2 * chunks], refs[2 * chunks + 1 :]
    held = slab_of(held_refs)
    held_halves = halves(held)
    total = total_refs[0][...] if totals else jnp.zeros(held.shape, jnp.float32)
    for user_ref, list_ref, errors_ref in zip(user_refs, list_refs, errors_refs):
        users = errors_ref.shape[1]
        user = halves(user_ref[:users, :])
        errors = errors_of(held_halves, user, *listed(list_ref, users, step, obs))
        errors_ref[...] = errors
        total += product(halves(errors), user, NN)
    out_ref[...] = kept() * held - LEARN_RATE * total


def users_kernel(pieces, chunks, *refs):
    held_refs, errors_refs, refs = refs[:pieces], refs[pieces : pieces + chunks], refs[pieces + chunks :]
    user_refs, out_refs = refs[:chunks], refs[chunks:]
    held = halves(slab_of(held_refs))
    for errors_ref, user_ref, out_ref in zip(errors_refs, user_refs, out_refs):
        step = product(halves(errors_ref[...]), held, TN)
        out_ref[...] = DECAY * user_ref[: out_ref.shape[0], :] - LEARN_RATE * step


def last_kernel(step, obs, pieces, chunks, *refs):
    held_refs, refs = refs[:pieces], refs[pieces:]
    user_refs, list_refs, out_ref, new_refs = refs[:chunks], refs[chunks : 2 * chunks], refs[2 * chunks], refs[2 * chunks + 1 :]
    held = slab_of(held_refs)
    held_halves = halves(held)
    total = jnp.zeros(held.shape, jnp.float32)
    for user_ref, list_ref, new_ref in zip(user_refs, list_refs, new_refs):
        user = user_ref[...]
        user_halves = halves(user)
        errors = errors_of(held_halves, user_halves, *listed(list_ref, user_ref.shape[0], step, obs))
        errors = halves(errors)
        total += product(errors, user_halves, NN)
        new_ref[...] = DECAY * user - LEARN_RATE * product(errors, held_halves, TN)
    out_ref[...] = kept() * held - LEARN_RATE * total


def share_kernel(parts_ref, out_ref):
    out_ref[...] = parts_ref[FIRST ^ parity()] + parts_ref[SECOND ^ parity()]


def home_kernel(share_ref, own_ref, a_ref, b_ref, c_ref, out_ref, share_out_ref):
    share_out_ref[...] = share_ref[...]
    place = lax.axis_index("split") ^ parity()
    for ref, places in zip((own_ref, a_ref, b_ref, c_ref), ((FIRST, SECOND), *HELPERS)):

        @pl.when((place == places[0]) | (place == places[1]))
        def _(ref=ref):
            out_ref[...] = ref[...]


def local(user_factors, item_factors, obs_items, obs_conf):
    slab, rank = item_factors.shape
    users = user_factors.shape[0]
    _, steps, obs = obs_items.shape
    n = lax.axis_size("split")
    blocks = lax.axis_size("blk")
    share_rows = slab // n
    chunks = 1 + len(HELPERS)
    items = jnp.transpose(obs_items, (1, 2, 0))
    conf = jnp.transpose(obs_conf, (1, 2, 0))
    both = ("blk", "split")

    def at(b, k):
        return b * n + (k ^ (b & 1))

    def fetch(x, helpers):
        pairs = [(at(b, h), at(b, w)) for b in range(blocks) for h, w in zip(helpers, (FIRST, SECOND))]
        return lax.ppermute(x, both, pairs)

    def give(x, helpers):
        pairs = [(at(b, w), at(b, h)) for b in range(blocks) for h, w in zip(helpers, (FIRST, SECOND))]
        return lax.ppermute(x, both, pairs)

    def onward(x):
        same, cross = [], []
        for b in range(blocks):
            for w, v in ((FIRST, SECOND), (SECOND, FIRST)):
                source = at((b + 1) % blocks, w)
                same.append((source, at(b, w)))
                cross.append((source, at(b, v)))
        return [lax.ppermute(x, both, same), lax.ppermute(x, both, cross)]

    hbm = pl.BlockSpec(memory_space=pltpu.HBM)
    lists_rows = steps * obs
    (own,) = call(
        pack_kernel,
        [(users + lists_rows, rank)],
        "pack",
        params=None,
        in_specs=[hbm] * 3,
        out_specs=[hbm],
        scratch_shapes=[pltpu.VMEM(items.shape, jnp.int32)] * 2
        + [pltpu.VMEM((users + lists_rows, rank), jnp.float32)]
        + [pltpu.SemaphoreType.DMA((PIECES + 2,)), pltpu.SemaphoreType.DMA((PIECES + 1,))],
    )(user_factors, items, conf)
    packs = [own] + [fetch(own, helpers) for helpers in HELPERS]
    user = packs
    held = [item_factors]
    for step in range(steps - 1):
        if step == 0:
            kernel = functools.partial(own_kernel, step, obs)
            own_errors, total = call(kernel, [(slab, users), (slab, rank)], "own")(item_factors, own)
            first, totals = [own_errors], [total]
        else:
            first, totals = [], []
        rest = chunks - len(first)
        kernel = functools.partial(group_kernel, step, obs, len(held), len(totals), rest)
        outs = [(slab, rank)] + [(slab, users)] * rest
        out, *errors = call(kernel, outs, "group")(*held, *totals, *user[-rest:], *packs[-rest:])
        sent = onward(out)
        kernel = functools.partial(users_kernel, len(held), chunks)
        user = call(kernel, [(users, rank)] * chunks, "users")(*held, *first, *errors, *user)
        held = sent
    kernel = functools.partial(last_kernel, steps - 1, obs, len(held), chunks)
    out, *user = call(kernel, [(slab, rank)] + [(users, rank)] * chunks, "last")(*held, *user, *packs)
    parts = lax.all_to_all(out.reshape(n, share_rows, rank), "split", 0, 0)
    early = pl.CostEstimate(flops=1 << 36, bytes_accessed=1 << 20, transcendentals=0)
    (share,) = call(share_kernel, [(share_rows, rank)], "share", cost_estimate=early)(parts)
    share = lax.ppermute(share, "blk", [((b + 1) % blocks, b) for b in range(blocks)])
    home = [give(u, helpers) for u, helpers in zip(user[1:], HELPERS)]
    outs = [(users, rank), (share_rows, rank)]
    user_out, share_out = call(home_kernel, outs, "home")(share, user[0], *home)
    return user_out, share_out


def solution(mesh):
    in_specs = (
        P(("blk", "split"), None),
        P("blk", None),
        P(("blk", "split"), None, None),
        P(("blk", "split"), None, None),
    )
    out_specs = (P(("blk", "split"), None), P(("blk", "split"), None))
    return jax.shard_map(local, mesh=mesh, in_specs=in_specs, out_specs=out_specs, check_vma=False)
```

```python
import functools

import jax
import jax.numpy as jnp
from jax import lax
from jax.experimental import pallas as pl
from jax.experimental.pallas import tpu as pltpu
from jax.sharding import PartitionSpec as P

LEARN_RATE = 0.0005
CONF_SCALE = 0.5
RIDGE_COEF = 0.01
DECAY = 1.0 - LEARN_RATE * RIDGE_COEF
PARAMS = pltpu.CompilerParams(vmem_limit_bytes=16 << 20)

NT = (((1,), (1,)), ((), ()))
NN = (((1,), (0,)), ((), ()))
TN = (((0,), (0,)), ((), ()))

FIRST, SECOND = 2, 7
HELPERS = ((0, 5), (4, 1), (3, 6))


def halves(x):
    high = x.astype(jnp.bfloat16)
    low = (x - high.astype(jnp.float32)).astype(jnp.bfloat16)
    return high, low


def product(a, b, dims):
    def one(p, q):
        return lax.dot_general(p, q, dims, preferred_element_type=jnp.float32)

    return one(a[0], b[0]) + (one(a[0], b[1]) + one(a[1], b[0]))


def weigh(items, conf, slab):
    rows = lax.broadcasted_iota(jnp.int32, (slab, items.shape[1]), 0)
    counts = jnp.zeros(rows.shape, jnp.float32)
    for k in range(items.shape[0]):
        counts += jnp.where(items[k : k + 1] == rows, conf[k : k + 1], 0.0)
    weights = 1.0 + CONF_SCALE * counts
    return weights, jnp.where(counts > 0.0, weights, 0.0)


def listed(ref, users, step, obs):
    at = users + step * obs
    return ref[at : at + obs, :users].astype(jnp.int32), ref[at : at + obs, users:]


def parity():
    return lax.axis_index("blk") & 1


def slab_of(refs):
    held = refs[0][...]
    for ref in refs[1:]:
        held += ref[...]
    return held


def call(kernel, outs, name, params=PARAMS, **kwargs):
    return pl.pallas_call(
        kernel,
        out_shape=[jax.ShapeDtypeStruct(shape, dtype) for shape, dtype in outs],
        compiler_params=params,
        name=name,
        **kwargs,
    )


def kept():
    return jnp.where((lax.axis_index("split") ^ parity()) == FIRST, DECAY, 0.0)


def first_kernel(user_hbm, held_hbm, items_hbm, conf_hbm, part_hbm, pack_hbm, user_ref, held_ref, items, conf, part, pack, sems):
    users = user_ref.shape[0]
    slab = held_ref.shape[0]
    steps, obs, _ = items.shape
    pairs = ((items_hbm, items), (conf_hbm, conf), (held_hbm, held_ref), (user_hbm, user_ref))
    loads = [pltpu.make_async_copy(source, target, sems.at[i]) for i, (source, target) in enumerate(pairs)]
    for copy in loads:
        copy.start()
    loads[0].wait()
    loads[1].wait()
    for s in range(steps):
        at = users + s * obs
        pack[at : at + obs, :users] = items[s].astype(jnp.float32)
        pack[at : at + obs, users:] = conf[s].astype(jnp.float32)
    weights, targets = weigh(items[0], conf[0].astype(jnp.float32), slab)
    loads[2].wait()
    loads[3].wait()
    held = held_ref[...]
    held_halves = halves(held)
    user = halves(user_ref[...])
    errors = halves(weights * product(held_halves, user, NT) - targets)
    part[...] = kept() * held - LEARN_RATE * product(errors, user, NN)
    send_part = pltpu.make_async_copy(part, part_hbm, sems.at[4])
    send_part.start()
    pack[:users, :] = DECAY * user_ref[...] - LEARN_RATE * product(errors, held_halves, TN)
    send_pack = pltpu.make_async_copy(pack, pack_hbm, sems.at[5])
    send_pack.start()
    send_part.wait()
    send_pack.wait()


def sum_kernel(*refs):
    refs[-1][...] = slab_of(refs[:-1])


def prepare_kernel(step, obs, chunks, *refs):
    pack_refs, out_refs = refs[:chunks], refs[chunks:]
    for i, pack_ref in enumerate(pack_refs):
        high_ref, low_ref, weights_ref, targets_ref = out_refs[4 * i : 4 * i + 4]
        users = high_ref.shape[0]
        high_ref[...], low_ref[...] = halves(pack_ref[:users, :])
        weights_ref[...], targets_ref[...] = weigh(*listed(pack_ref, users, step, obs), weights_ref.shape[0])


def group_kernel(pieces, chunks, *refs):
    held_refs, ready_refs, out_ref, errors_refs = refs[:pieces], refs[pieces : pieces + 4 * chunks], refs[pieces + 4 * chunks], refs[pieces + 4 * chunks + 1 :]
    held = slab_of(held_refs)
    held_halves = halves(held)
    total = jnp.zeros(held.shape, jnp.float32)
    for i in range(chunks):
        high_ref, low_ref, weights_ref, targets_ref = ready_refs[4 * i : 4 * i + 4]
        user = high_ref[...], low_ref[...]
        errors = halves(weights_ref[...] * product(held_halves, user, NT) - targets_ref[...])
        errors_refs[2 * i][...], errors_refs[2 * i + 1][...] = errors
        total += product(errors, user, NN)
    out_ref[...] = kept() * held - LEARN_RATE * total


def users_kernel(step, obs, pieces, chunks, *refs):
    held_refs, errors_refs, refs = refs[:pieces], refs[pieces : pieces + 2 * chunks], refs[pieces + 2 * chunks :]
    user_refs, pack_refs, out_refs = refs[:chunks], refs[chunks : 2 * chunks], refs[2 * chunks :]
    held = halves(slab_of(held_refs))
    for i in range(chunks):
        out_ref, high_ref, low_ref, weights_ref, targets_ref = out_refs[5 * i : 5 * i + 5]
        users = out_ref.shape[0]
        move = product((errors_refs[2 * i][...], errors_refs[2 * i + 1][...]), held, TN)
        new = DECAY * user_refs[i][:users, :] - LEARN_RATE * move
        out_ref[...] = new
        high_ref[...], low_ref[...] = halves(new)
        weights_ref[...], targets_ref[...] = weigh(*listed(pack_refs[i], users, step + 1, obs), weights_ref.shape[0])


def last_kernel(pieces, chunks, *refs):
    held_refs, ready_refs, refs = refs[:pieces], refs[pieces : pieces + 4 * chunks], refs[pieces + 4 * chunks :]
    user_refs, out_ref, new_refs = refs[:chunks], refs[chunks], refs[chunks + 1 :]
    held = slab_of(held_refs)
    held_halves = halves(held)
    total = jnp.zeros(held.shape, jnp.float32)
    for i in range(chunks):
        high_ref, low_ref, weights_ref, targets_ref = ready_refs[4 * i : 4 * i + 4]
        user = high_ref[...], low_ref[...]
        errors = halves(weights_ref[...] * product(held_halves, user, NT) - targets_ref[...])
        total += product(errors, user, NN)
        new_refs[i][...] = DECAY * user_refs[i][...] - LEARN_RATE * product(errors, held_halves, TN)
    out_ref[...] = kept() * held - LEARN_RATE * total


def share_kernel(parts_ref, out_ref):
    out_ref[...] = parts_ref[FIRST ^ parity()] + parts_ref[SECOND ^ parity()]


def home_kernel(share_ref, own_ref, a_ref, b_ref, c_ref, out_ref, share_out_ref):
    share_out_ref[...] = share_ref[...]
    place = lax.axis_index("split") ^ parity()
    for ref, places in zip((own_ref, a_ref, b_ref, c_ref), ((FIRST, SECOND), *HELPERS)):

        @pl.when((place == places[0]) | (place == places[1]))
        def _(ref=ref):
            out_ref[...] = ref[...]


def local(user_factors, item_factors, obs_items, obs_conf):
    slab, rank = item_factors.shape
    users = user_factors.shape[0]
    _, steps, obs = obs_items.shape
    n = lax.axis_size("split")
    blocks = lax.axis_size("blk")
    share_rows = slab // n
    chunks = 1 + len(HELPERS)
    items = jnp.transpose(obs_items, (1, 2, 0))
    conf = jnp.transpose(obs_conf, (1, 2, 0))
    both = ("blk", "split")

    def at(b, k):
        return b * n + (k ^ (b & 1))

    def fetch(x, helpers):
        pairs = [(at(b, h), at(b, w)) for b in range(blocks) for h, w in zip(helpers, (FIRST, SECOND))]
        return lax.ppermute(x, both, pairs)

    def give(x, helpers):
        pairs = [(at(b, w), at(b, h)) for b in range(blocks) for h, w in zip(helpers, (FIRST, SECOND))]
        return lax.ppermute(x, both, pairs)

    def onward(x):
        pairs = [(at((b + 1) % blocks, w), at(b, w)) for b in range(blocks) for w in (FIRST, SECOND)]
        same = lax.ppermute(x, both, pairs)
        pairs = [(at(b, w), at(b, v)) for b in range(blocks) for w, v in ((FIRST, SECOND), (SECOND, FIRST))]
        return [same, lax.ppermute(same, both, pairs)]

    f32, bf16 = jnp.float32, jnp.bfloat16
    hbm = pl.BlockSpec(memory_space=pltpu.HBM)
    rows = users + steps * obs
    part, pack = call(
        first_kernel,
        [((slab, rank), f32), ((rows, rank), f32)],
        "first",
        params=None,
        in_specs=[hbm] * 4,
        out_specs=[hbm] * 2,
        scratch_shapes=[pltpu.VMEM(user_factors.shape, f32), pltpu.VMEM(item_factors.shape, f32)]
        + [pltpu.VMEM(items.shape, jnp.int32)] * 2
        + [pltpu.VMEM((slab, rank), f32), pltpu.VMEM((rows, rank), f32), pltpu.SemaphoreType.DMA((6,))],
    )(user_factors, item_factors, items, conf)
    arrived = [part] + [fetch(part, helpers) for helpers in HELPERS]
    packs = [pack] + [fetch(pack, helpers) for helpers in HELPERS]
    (out,) = call(sum_kernel, [((slab, rank), f32)], "sum")(*arrived)
    held = onward(out)
    factors, half, square = ((users, rank), f32), ((users, rank), bf16), ((slab, users), f32)
    pieces = len(held)
    ready = [half, half, square, square]
    kernel = functools.partial(prepare_kernel, 1, obs, chunks)
    ahead = call(kernel, ready * chunks, "prepare")(*packs)
    user = packs
    for step in range(1, steps - 1):
        kernel = functools.partial(group_kernel, pieces, chunks)
        outs = [((slab, rank), f32)] + [((slab, users), bf16)] * (2 * chunks)
        out, *errors = call(kernel, outs, "group")(*held, *ahead)
        sent = onward(out)
        kernel = functools.partial(users_kernel, step, obs, pieces, chunks)
        outs = call(kernel, [factors, *ready] * chunks, "users")(*held, *errors, *user, *packs)
        user = outs[::5]
        ahead = [x for i, x in enumerate(outs) if i % 5]
        held = sent
    kernel = functools.partial(last_kernel, pieces, chunks)
    out, *user = call(kernel, [((slab, rank), f32)] + [factors] * chunks, "last")(*held, *ahead, *user)
    parts = lax.all_to_all(out.reshape(n, share_rows, rank), "split", 0, 0)
    early = pl.CostEstimate(flops=1 << 36, bytes_accessed=1 << 20, transcendentals=0)
    (share,) = call(share_kernel, [((share_rows, rank), f32)], "share", cost_estimate=early)(parts)
    share = lax.ppermute(share, "blk", [((b + 1) % blocks, b) for b in range(blocks)])
    home = [give(u, helpers) for u, helpers in zip(user[1:], HELPERS)]
    outs = [factors, ((share_rows, rank), f32)]
    user_out, share_out = call(home_kernel, outs, "home")(share, user[0], *home)
    return user_out, share_out


def solution(mesh):
    in_specs = (
        P(("blk", "split"), None),
        P("blk", None),
        P(("blk", "split"), None, None),
        P(("blk", "split"), None, None),
    )
    out_specs = (P(("blk", "split"), None), P(("blk", "split"), None))
    return jax.shard_map(local, mesh=mesh, in_specs=in_specs, out_specs=out_specs, check_vma=False)
```

```python
import functools

import jax
import jax.numpy as jnp
from jax import lax
from jax.experimental import pallas as pl
from jax.experimental.pallas import tpu as pltpu
from jax.sharding import PartitionSpec as P

LEARN_RATE = 0.0005
CONF_SCALE = 0.5
RIDGE_COEF = 0.01
DECAY = 1.0 - LEARN_RATE * RIDGE_COEF
PARAMS = pltpu.CompilerParams(vmem_limit_bytes=16 << 20)

NT = (((1,), (1,)), ((), ()))
NN = (((1,), (0,)), ((), ()))
TN = (((0,), (0,)), ((), ()))

FIRST, SECOND = 2, 7
HELPERS = ((0, 5), (4, 1), (3, 6))


def halves(x):
    high = x.astype(jnp.bfloat16)
    low = (x - high.astype(jnp.float32)).astype(jnp.bfloat16)
    return high, low


def product(a, b, dims):
    def one(p, q):
        return lax.dot_general(p, q, dims, preferred_element_type=jnp.float32)

    return one(a[0], b[0]) + (one(a[0], b[1]) + one(a[1], b[0]))


def weigh(items, conf, slab):
    rows = lax.broadcasted_iota(jnp.int32, (slab, items.shape[1]), 0)
    counts = jnp.zeros(rows.shape, jnp.float32)
    for k in range(items.shape[0]):
        counts += jnp.where(items[k : k + 1] == rows, conf[k : k + 1], 0.0)
    weights = 1.0 + CONF_SCALE * counts
    return weights, jnp.where(counts > 0.0, weights, 0.0)


def listed(ref, users, step, obs):
    at = users + step * obs
    return ref[at : at + obs, :users].astype(jnp.int32), ref[at : at + obs, users:]


def parity():
    return lax.axis_index("blk") & 1


def slab_of(refs):
    held = refs[0][...]
    for ref in refs[1:]:
        held += ref[...]
    return held


def call(kernel, outs, name, params=PARAMS, **kwargs):
    return pl.pallas_call(
        kernel,
        out_shape=[jax.ShapeDtypeStruct(shape, dtype) for shape, dtype in outs],
        compiler_params=params,
        name=name,
        **kwargs,
    )


def kept():
    return jnp.where((lax.axis_index("split") ^ parity()) == FIRST, DECAY, 0.0)


def first_kernel(user_hbm, held_hbm, items_hbm, conf_hbm, part_hbm, pack_hbm, user_ref, held_ref, items, conf, part, pack, sems):
    users = user_ref.shape[0]
    slab = held_ref.shape[0]
    steps, obs, _ = items.shape
    pairs = ((items_hbm, items), (conf_hbm, conf), (held_hbm, held_ref), (user_hbm, user_ref))
    loads = [pltpu.make_async_copy(source, target, sems.at[i]) for i, (source, target) in enumerate(pairs)]
    for copy in loads:
        copy.start()
    loads[0].wait()
    loads[1].wait()
    for s in range(steps):
        at = users + s * obs
        pack[at : at + obs, :users] = items[s].astype(jnp.float32)
        pack[at : at + obs, users:] = conf[s].astype(jnp.float32)
    weights, targets = weigh(items[0], conf[0].astype(jnp.float32), slab)
    loads[2].wait()
    loads[3].wait()
    held = held_ref[...]
    held_halves = halves(held)
    user = halves(user_ref[...])
    errors = halves(weights * product(held_halves, user, NT) - targets)
    part[...] = kept() * held - LEARN_RATE * product(errors, user, NN)
    send_part = pltpu.make_async_copy(part, part_hbm, sems.at[4])
    send_part.start()
    pack[:users, :] = DECAY * user_ref[...] - LEARN_RATE * product(errors, held_halves, TN)
    send_pack = pltpu.make_async_copy(pack, pack_hbm, sems.at[5])
    send_pack.start()
    send_part.wait()
    send_pack.wait()


def sum_kernel(*refs):
    refs[-1][...] = slab_of(refs[:-1])


def prepare_kernel(step, obs, chunks, *refs):
    pack_refs, out_refs = refs[:chunks], refs[chunks:]
    for i, pack_ref in enumerate(pack_refs):
        high_ref, low_ref, weights_ref, targets_ref = out_refs[4 * i : 4 * i + 4]
        users = high_ref.shape[0]
        high_ref[...], low_ref[...] = halves(pack_ref[:users, :])
        weights_ref[...], targets_ref[...] = weigh(*listed(pack_ref, users, step, obs), weights_ref.shape[0])


def group_kernel(pieces, chunks, *refs):
    held_refs, ready_refs, out_ref, errors_refs = refs[:pieces], refs[pieces : pieces + 4 * chunks], refs[pieces + 4 * chunks], refs[pieces + 4 * chunks + 1 :]
    held = slab_of(held_refs)
    held_halves = halves(held)
    total = jnp.zeros(held.shape, jnp.float32)
    for i in range(chunks):
        high_ref, low_ref, weights_ref, targets_ref = ready_refs[4 * i : 4 * i + 4]
        user = high_ref[...], low_ref[...]
        errors = halves(weights_ref[...] * product(held_halves, user, NT) - targets_ref[...])
        errors_refs[2 * i][...], errors_refs[2 * i + 1][...] = errors
        total += product(errors, user, NN)
    out_ref[...] = kept() * held - LEARN_RATE * total


def users_kernel(step, obs, pieces, chunks, *refs):
    held_refs, errors_refs, refs = refs[:pieces], refs[pieces : pieces + 2 * chunks], refs[pieces + 2 * chunks :]
    user_refs, pack_refs, out_refs = refs[:chunks], refs[chunks : 2 * chunks], refs[2 * chunks :]
    held = halves(slab_of(held_refs))
    for i in range(chunks):
        out_ref, high_ref, low_ref, weights_ref, targets_ref = out_refs[5 * i : 5 * i + 5]
        users = out_ref.shape[0]
        move = product((errors_refs[2 * i][...], errors_refs[2 * i + 1][...]), held, TN)
        new = DECAY * user_refs[i][:users, :] - LEARN_RATE * move
        out_ref[...] = new
        high_ref[...], low_ref[...] = halves(new)
        weights_ref[...], targets_ref[...] = weigh(*listed(pack_refs[i], users, step + 1, obs), weights_ref.shape[0])


def last_kernel(pieces, chunks, *refs):
    held_refs, ready_refs, refs = refs[:pieces], refs[pieces : pieces + 4 * chunks], refs[pieces + 4 * chunks :]
    user_refs, out_ref, new_refs = refs[:chunks], refs[chunks], refs[chunks + 1 :]
    held = slab_of(held_refs)
    held_halves = halves(held)
    total = jnp.zeros(held.shape, jnp.float32)
    for i in range(chunks):
        high_ref, low_ref, weights_ref, targets_ref = ready_refs[4 * i : 4 * i + 4]
        user = high_ref[...], low_ref[...]
        errors = halves(weights_ref[...] * product(held_halves, user, NT) - targets_ref[...])
        total += product(errors, user, NN)
        new_refs[i][...] = DECAY * user_refs[i][...] - LEARN_RATE * product(errors, held_halves, TN)
    out_ref[...] = kept() * held - LEARN_RATE * total


def share_kernel(parts_ref, out_ref):
    out_ref[...] = parts_ref[FIRST ^ parity()] + parts_ref[SECOND ^ parity()]


def home_kernel(share_ref, own_ref, a_ref, b_ref, c_ref, out_ref, share_out_ref):
    share_out_ref[...] = share_ref[...]
    place = lax.axis_index("split") ^ parity()
    for ref, places in zip((own_ref, a_ref, b_ref, c_ref), ((FIRST, SECOND), *HELPERS)):

        @pl.when((place == places[0]) | (place == places[1]))
        def _(ref=ref):
            out_ref[...] = ref[...]


def local(user_factors, item_factors, obs_items, obs_conf):
    slab, rank = item_factors.shape
    users = user_factors.shape[0]
    _, steps, obs = obs_items.shape
    n = lax.axis_size("split")
    blocks = lax.axis_size("blk")
    share_rows = slab // n
    chunks = 1 + len(HELPERS)
    items = jnp.transpose(obs_items, (1, 2, 0))
    conf = jnp.transpose(obs_conf, (1, 2, 0))
    both = ("blk", "split")

    def at(b, k):
        return b * n + (k ^ (b & 1))

    def fetch(x, helpers):
        pairs = [(at(b, h), at(b, w)) for b in range(blocks) for h, w in zip(helpers, (FIRST, SECOND))]
        return lax.ppermute(x, both, pairs)

    def give(x, helpers):
        pairs = [(at(b, w), at(b, h)) for b in range(blocks) for h, w in zip(helpers, (FIRST, SECOND))]
        return lax.ppermute(x, both, pairs)

    def onward(x):
        same, cross = [], []
        for b in range(blocks):
            for w, v in ((FIRST, SECOND), (SECOND, FIRST)):
                source = at((b + 1) % blocks, w)
                same.append((source, at(b, w)))
                cross.append((source, at(b, v)))
        return [lax.ppermute(x, both, same), lax.ppermute(x, both, cross)]

    f32, bf16 = jnp.float32, jnp.bfloat16
    early = pl.CostEstimate(flops=1 << 36, bytes_accessed=1 << 20, transcendentals=0)
    hbm = pl.BlockSpec(memory_space=pltpu.HBM)
    rows = users + steps * obs
    part, pack = call(
        first_kernel,
        [((slab, rank), f32), ((rows, rank), f32)],
        "first",
        params=None,
        in_specs=[hbm] * 4,
        out_specs=[hbm] * 2,
        scratch_shapes=[pltpu.VMEM(user_factors.shape, f32), pltpu.VMEM(item_factors.shape, f32)]
        + [pltpu.VMEM(items.shape, jnp.int32)] * 2
        + [pltpu.VMEM((slab, rank), f32), pltpu.VMEM((rows, rank), f32), pltpu.SemaphoreType.DMA((6,))],
    )(user_factors, item_factors, items, conf)
    arrived = [part] + [fetch(part, helpers) for helpers in HELPERS]
    packs = [pack] + [fetch(pack, helpers) for helpers in HELPERS]
    (out,) = call(sum_kernel, [((slab, rank), f32)], "sum", cost_estimate=early)(*arrived)
    held = onward(out)
    factors, half, square = ((users, rank), f32), ((users, rank), bf16), ((slab, users), f32)
    pieces = len(held)
    ready = [half, half, square, square]
    kernel = functools.partial(prepare_kernel, 1, obs, chunks)
    ahead = call(kernel, ready * chunks, "prepare")(*packs)
    user = packs
    for step in range(1, steps - 1):
        kernel = functools.partial(group_kernel, pieces, chunks)
        outs = [((slab, rank), f32)] + [((slab, users), bf16)] * (2 * chunks)
        out, *errors = call(kernel, outs, "group")(*held, *ahead)
        sent = onward(out)
        kernel = functools.partial(users_kernel, step, obs, pieces, chunks)
        outs = call(kernel, [factors, *ready] * chunks, "users")(*held, *errors, *user, *packs)
        user = outs[::5]
        ahead = [x for i, x in enumerate(outs) if i % 5]
        held = sent
    kernel = functools.partial(last_kernel, pieces, chunks)
    out, *user = call(kernel, [((slab, rank), f32)] + [factors] * chunks, "last")(*held, *ahead, *user)
    parts = lax.all_to_all(out.reshape(n, share_rows, rank), "split", 0, 0)
    (share,) = call(share_kernel, [((share_rows, rank), f32)], "share", cost_estimate=early)(parts)
    share = lax.ppermute(share, "blk", [((b + 1) % blocks, b) for b in range(blocks)])
    home = [give(u, helpers) for u, helpers in zip(user[1:], HELPERS)]
    outs = [factors, ((share_rows, rank), f32)]
    user_out, share_out = call(home_kernel, outs, "home")(share, user[0], *home)
    return user_out, share_out


def solution(mesh):
    in_specs = (
        P(("blk", "split"), None),
        P("blk", None),
        P(("blk", "split"), None, None),
        P(("blk", "split"), None, None),
    )
    out_specs = (P(("blk", "split"), None), P(("blk", "split"), None))
    return jax.shard_map(local, mesh=mesh, in_specs=in_specs, out_specs=out_specs, check_vma=False)
```

```python
import functools

import jax
import jax.numpy as jnp
from jax import lax
from jax.experimental import pallas as pl
from jax.experimental.pallas import tpu as pltpu
from jax.sharding import PartitionSpec as P

LEARN_RATE = 0.0005
CONF_SCALE = 0.5
RIDGE_COEF = 0.01
DECAY = 1.0 - LEARN_RATE * RIDGE_COEF
PARAMS = pltpu.CompilerParams(vmem_limit_bytes=16 << 20)

NT = (((1,), (1,)), ((), ()))
NN = (((1,), (0,)), ((), ()))
TN = (((0,), (0,)), ((), ()))

FIRST, SECOND = 2, 7
HELPERS = ((0, 5), (4, 1), (3, 6))


def halves(x):
    high = x.astype(jnp.bfloat16)
    low = (x - high.astype(jnp.float32)).astype(jnp.bfloat16)
    return high, low


def product(a, b, dims):
    def one(p, q):
        return lax.dot_general(p, q, dims, preferred_element_type=jnp.float32)

    return one(a[0], b[0]) + (one(a[0], b[1]) + one(a[1], b[0]))


def weigh(items, conf, slab):
    rows = lax.broadcasted_iota(jnp.int32, (slab, items.shape[1]), 0)
    counts = jnp.zeros(rows.shape, jnp.float32)
    for k in range(items.shape[0]):
        counts += jnp.where(items[k : k + 1] == rows, conf[k : k + 1], 0.0)
    weights = 1.0 + CONF_SCALE * counts
    return weights, jnp.where(counts > 0.0, weights, 0.0)


def listed(ref, users, step, obs):
    at = users + step * obs
    return ref[at : at + obs, :users].astype(jnp.int32), ref[at : at + obs, users:]


def parity():
    return lax.axis_index("blk") & 1


def slab_of(refs):
    held = refs[0][...]
    for ref in refs[1:]:
        held += ref[...]
    return held


def call(kernel, outs, name, params=PARAMS, **kwargs):
    return pl.pallas_call(
        kernel,
        out_shape=[jax.ShapeDtypeStruct(shape, dtype) for shape, dtype in outs],
        compiler_params=params,
        name=name,
        **kwargs,
    )


def kept():
    return jnp.where((lax.axis_index("split") ^ parity()) == FIRST, DECAY, 0.0)


def first_kernel(user_hbm, held_hbm, items_hbm, conf_hbm, part, pack, user_ref, held_ref, items, conf, sems):
    users = user_ref.shape[0]
    slab = held_ref.shape[0]
    steps, obs, _ = items.shape
    pairs = ((items_hbm, items), (conf_hbm, conf), (held_hbm, held_ref), (user_hbm, user_ref))
    loads = [pltpu.make_async_copy(source, target, sems.at[i]) for i, (source, target) in enumerate(pairs)]
    for copy in loads:
        copy.start()
    loads[0].wait()
    loads[1].wait()
    for s in range(steps):
        at = users + s * obs
        pack[at : at + obs, :users] = items[s].astype(jnp.float32)
        pack[at : at + obs, users:] = conf[s].astype(jnp.float32)
    weights, targets = weigh(items[0], conf[0].astype(jnp.float32), slab)
    loads[2].wait()
    loads[3].wait()
    held = held_ref[...]
    held_halves = halves(held)
    user = halves(user_ref[...])
    errors = halves(weights * product(held_halves, user, NT) - targets)
    part[...] = kept() * held - LEARN_RATE * product(errors, user, NN)
    pack[:users, :] = DECAY * user_ref[...] - LEARN_RATE * product(errors, held_halves, TN)


def sum_kernel(*refs):
    refs[-1][...] = slab_of(refs[:-1])


def prepare_kernel(step, obs, chunks, *refs):
    pack_refs, out_refs = refs[:chunks], refs[chunks:]
    for i, pack_ref in enumerate(pack_refs):
        high_ref, low_ref, weights_ref, targets_ref = out_refs[4 * i : 4 * i + 4]
        users = high_ref.shape[0]
        high_ref[...], low_ref[...] = halves(pack_ref[:users, :])
        weights_ref[...], targets_ref[...] = weigh(*listed(pack_ref, users, step, obs), weights_ref.shape[0])


def group_kernel(pieces, chunks, *refs):
    held_refs, ready_refs, out_ref, errors_refs = refs[:pieces], refs[pieces : pieces + 4 * chunks], refs[pieces + 4 * chunks], refs[pieces + 4 * chunks + 1 :]
    held = slab_of(held_refs)
    held_halves = halves(held)
    total = jnp.zeros(held.shape, jnp.float32)
    for i in range(chunks):
        high_ref, low_ref, weights_ref, targets_ref = ready_refs[4 * i : 4 * i + 4]
        user = high_ref[...], low_ref[...]
        errors = halves(weights_ref[...] * product(held_halves, user, NT) - targets_ref[...])
        errors_refs[2 * i][...], errors_refs[2 * i + 1][...] = errors
        total += product(errors, user, NN)
    out_ref[...] = kept() * held - LEARN_RATE * total


def users_kernel(step, obs, pieces, chunks, *refs):
    held_refs, errors_refs, refs = refs[:pieces], refs[pieces : pieces + 2 * chunks], refs[pieces + 2 * chunks :]
    user_refs, pack_refs, out_refs = refs[:chunks], refs[chunks : 2 * chunks], refs[2 * chunks :]
    held = halves(slab_of(held_refs))
    for i in range(chunks):
        out_ref, high_ref, low_ref, weights_ref, targets_ref = out_refs[5 * i : 5 * i + 5]
        users = out_ref.shape[0]
        move = product((errors_refs[2 * i][...], errors_refs[2 * i + 1][...]), held, TN)
        new = DECAY * user_refs[i][:users, :] - LEARN_RATE * move
        out_ref[...] = new
        high_ref[...], low_ref[...] = halves(new)
        weights_ref[...], targets_ref[...] = weigh(*listed(pack_refs[i], users, step + 1, obs), weights_ref.shape[0])


def last_kernel(pieces, chunks, *refs):
    held_refs, ready_refs, refs = refs[:pieces], refs[pieces : pieces + 4 * chunks], refs[pieces + 4 * chunks :]
    user_refs, out_ref, new_refs = refs[:chunks], refs[chunks], refs[chunks + 1 :]
    held = slab_of(held_refs)
    held_halves = halves(held)
    total = jnp.zeros(held.shape, jnp.float32)
    for i in range(chunks):
        high_ref, low_ref, weights_ref, targets_ref = ready_refs[4 * i : 4 * i + 4]
        user = high_ref[...], low_ref[...]
        errors = halves(weights_ref[...] * product(held_halves, user, NT) - targets_ref[...])
        total += product(errors, user, NN)
        new_refs[i][...] = DECAY * user_refs[i][...] - LEARN_RATE * product(errors, held_halves, TN)
    out_ref[...] = kept() * held - LEARN_RATE * total


def share_kernel(parts_ref, out_ref):
    out_ref[...] = parts_ref[FIRST ^ parity()] + parts_ref[SECOND ^ parity()]


def home_kernel(share_ref, own_ref, a_ref, b_ref, c_ref, out_ref, share_out_ref):
    share_out_ref[...] = share_ref[...]
    place = lax.axis_index("split") ^ parity()
    for ref, places in zip((own_ref, a_ref, b_ref, c_ref), ((FIRST, SECOND), *HELPERS)):

        @pl.when((place == places[0]) | (place == places[1]))
        def _(ref=ref):
            out_ref[...] = ref[...]


def local(user_factors, item_factors, obs_items, obs_conf):
    slab, rank = item_factors.shape
    users = user_factors.shape[0]
    _, steps, obs = obs_items.shape
    n = lax.axis_size("split")
    blocks = lax.axis_size("blk")
    share_rows = slab // n
    chunks = 1 + len(HELPERS)
    items = jnp.transpose(obs_items, (1, 2, 0))
    conf = jnp.transpose(obs_conf, (1, 2, 0))
    both = ("blk", "split")

    def at(b, k):
        return b * n + (k ^ (b & 1))

    def fetch(x, helpers):
        pairs = [(at(b, h), at(b, w)) for b in range(blocks) for h, w in zip(helpers, (FIRST, SECOND))]
        return lax.ppermute(x, both, pairs)

    def give(x, helpers):
        pairs = [(at(b, w), at(b, h)) for b in range(blocks) for h, w in zip(helpers, (FIRST, SECOND))]
        return lax.ppermute(x, both, pairs)

    def onward(x):
        same, cross = [], []
        for b in range(blocks):
            for w, v in ((FIRST, SECOND), (SECOND, FIRST)):
                source = at((b + 1) % blocks, w)
                same.append((source, at(b, w)))
                cross.append((source, at(b, v)))
        return [lax.ppermute(x, both, cross), lax.ppermute(x, both, same)]

    f32, bf16 = jnp.float32, jnp.bfloat16
    early = pl.CostEstimate(flops=1 << 36, bytes_accessed=1 << 20, transcendentals=0)
    hbm = pl.BlockSpec(memory_space=pltpu.HBM)
    rows = users + steps * obs
    part, pack = call(
        first_kernel,
        [((slab, rank), f32), ((rows, rank), f32)],
        "first",
        in_specs=[hbm] * 4,
        scratch_shapes=[pltpu.VMEM(user_factors.shape, f32), pltpu.VMEM(item_factors.shape, f32)]
        + [pltpu.VMEM(items.shape, jnp.int32)] * 2
        + [pltpu.SemaphoreType.DMA((4,))],
    )(*[pltpu.with_memory_space_constraint(x, pltpu.HBM) for x in (user_factors, item_factors, items, conf)])
    arrived = [part] + [fetch(part, helpers) for helpers in HELPERS]
    packs = [pack] + [fetch(pack, helpers) for helpers in HELPERS]
    (out,) = call(sum_kernel, [((slab, rank), f32)], "sum", cost_estimate=early)(*arrived)
    held = onward(out)
    factors, half, square = ((users, rank), f32), ((users, rank), bf16), ((slab, users), f32)
    pieces = len(held)
    ready = [half, half, square, square]
    kernel = functools.partial(prepare_kernel, 1, obs, chunks)
    ahead = call(kernel, ready * chunks, "prepare")(*packs)
    user = packs
    for step in range(1, steps - 1):
        kernel = functools.partial(group_kernel, pieces, chunks)
        outs = [((slab, rank), f32)] + [((slab, users), bf16)] * (2 * chunks)
        out, *errors = call(kernel, outs, "group")(*held, *ahead)
        sent = onward(out)
        kernel = functools.partial(users_kernel, step, obs, pieces, chunks)
        outs = call(kernel, [factors, *ready] * chunks, "users")(*held, *errors, *user, *packs)
        user = outs[::5]
        ahead = [x for i, x in enumerate(outs) if i % 5]
        held = sent
    kernel = functools.partial(last_kernel, pieces, chunks)
    out, *user = call(kernel, [((slab, rank), f32)] + [factors] * chunks, "last")(*held, *ahead, *user)
    parts = lax.all_to_all(out.reshape(n, share_rows, rank), "split", 0, 0)
    (share,) = call(share_kernel, [((share_rows, rank), f32)], "share", cost_estimate=early)(parts)
    share = lax.ppermute(share, "blk", [((b + 1) % blocks, b) for b in range(blocks)])
    home = [give(u, helpers) for u, helpers in zip(user[1:], HELPERS)]
    outs = [factors, ((share_rows, rank), f32)]
    user_out, share_out = call(home_kernel, outs, "home")(share, user[0], *home)
    return user_out, share_out


def solution(mesh):
    in_specs = (
        P(("blk", "split"), None),
        P("blk", None),
        P(("blk", "split"), None, None),
        P(("blk", "split"), None, None),
    )
    out_specs = (P(("blk", "split"), None), P(("blk", "split"), None))
    return jax.shard_map(local, mesh=mesh, in_specs=in_specs, out_specs=out_specs, check_vma=False)
```

```python
import functools

import jax
import jax.numpy as jnp
from jax import lax
from jax.experimental import pallas as pl
from jax.experimental.pallas import tpu as pltpu
from jax.sharding import PartitionSpec as P

LEARN_RATE = 0.0005
CONF_SCALE = 0.5
RIDGE_COEF = 0.01
DECAY = 1.0 - LEARN_RATE * RIDGE_COEF
PARAMS = pltpu.CompilerParams(vmem_limit_bytes=16 << 20)

NT = (((1,), (1,)), ((), ()))
NN = (((1,), (0,)), ((), ()))
TN = (((0,), (0,)), ((), ()))

FIRST, SECOND = 2, 7
HELPERS = ((0, 5), (4, 1), (3, 6))


def halves(x):
    high = x.astype(jnp.bfloat16)
    low = (x - high.astype(jnp.float32)).astype(jnp.bfloat16)
    return high, low


def product(a, b, dims):
    def one(p, q):
        return lax.dot_general(p, q, dims, preferred_element_type=jnp.float32)

    if dims == TN:
        return one(a[0], b[0]) + (one(a[0], b[1]) + one(a[1], b[0]))
    rows = a[0].shape[0]
    stacked = one(jnp.concatenate(a, axis=0), b[0])
    return stacked[:rows] + (stacked[rows:] + one(a[0], b[1]))


def weigh(items, conf, slab):
    rows = lax.broadcasted_iota(jnp.int32, (slab, items.shape[1]), 0)
    counts = jnp.zeros(rows.shape, jnp.float32)
    for k in range(items.shape[0]):
        counts += jnp.where(items[k : k + 1] == rows, conf[k : k + 1], 0.0)
    weights = 1.0 + CONF_SCALE * counts
    return weights, jnp.where(counts > 0.0, weights, 0.0)


def listed(ref, users, step, obs):
    at = users + step * obs
    return ref[at : at + obs, :users].astype(jnp.int32), ref[at : at + obs, users:]


def parity():
    return lax.axis_index("blk") & 1


def slab_of(refs):
    held = refs[0][...]
    for ref in refs[1:]:
        held += ref[...]
    return held


def call(kernel, outs, name, params=PARAMS, **kwargs):
    return pl.pallas_call(
        kernel,
        out_shape=[jax.ShapeDtypeStruct(shape, dtype) for shape, dtype in outs],
        compiler_params=params,
        name=name,
        **kwargs,
    )


def kept():
    return jnp.where((lax.axis_index("split") ^ parity()) == FIRST, DECAY, 0.0)


def first_kernel(user_hbm, held_hbm, items_hbm, conf_hbm, part, pack, user_ref, held_ref, items, conf, sems):
    users = user_ref.shape[0]
    slab = held_ref.shape[0]
    steps, obs, _ = items.shape
    pairs = ((items_hbm, items), (conf_hbm, conf), (held_hbm, held_ref), (user_hbm, user_ref))
    loads = [pltpu.make_async_copy(source, target, sems.at[i]) for i, (source, target) in enumerate(pairs)]
    for copy in loads:
        copy.start()
    loads[0].wait()
    loads[1].wait()
    for s in range(steps):
        at = users + s * obs
        pack[at : at + obs, :users] = items[s].astype(jnp.float32)
        pack[at : at + obs, users:] = conf[s].astype(jnp.float32)
    weights, targets = weigh(items[0], conf[0].astype(jnp.float32), slab)
    loads[2].wait()
    loads[3].wait()
    held = held_ref[...]
    held_halves = halves(held)
    user = halves(user_ref[...])
    errors = halves(weights * product(held_halves, user, NT) - targets)
    part[...] = kept() * held - LEARN_RATE * product(errors, user, NN)
    pack[:users, :] = DECAY * user_ref[...] - LEARN_RATE * product(errors, held_halves, TN)


def sum_kernel(*refs):
    refs[-1][...] = slab_of(refs[:-1])


def prepare_kernel(step, obs, chunks, *refs):
    pack_refs, out_refs = refs[:chunks], refs[chunks:]
    for i, pack_ref in enumerate(pack_refs):
        high_ref, low_ref, weights_ref, targets_ref = out_refs[4 * i : 4 * i + 4]
        users = high_ref.shape[0]
        high_ref[...], low_ref[...] = halves(pack_ref[:users, :])
        weights_ref[...], targets_ref[...] = weigh(*listed(pack_ref, users, step, obs), weights_ref.shape[0])


def group_kernel(pieces, chunks, *refs):
    held_refs, ready_refs, out_ref, errors_refs = refs[:pieces], refs[pieces : pieces + 4 * chunks], refs[pieces + 4 * chunks], refs[pieces + 4 * chunks + 1 :]
    held = slab_of(held_refs)
    held_halves = halves(held)
    total = jnp.zeros(held.shape, jnp.float32)
    for i in range(chunks):
        high_ref, low_ref, weights_ref, targets_ref = ready_refs[4 * i : 4 * i + 4]
        user = high_ref[...], low_ref[...]
        errors = halves(weights_ref[...] * product(held_halves, user, NT) - targets_ref[...])
        errors_refs[2 * i][...], errors_refs[2 * i + 1][...] = errors
        total += product(errors, user, NN)
    out_ref[...] = kept() * held - LEARN_RATE * total


def users_kernel(step, obs, pieces, chunks, *refs):
    held_refs, errors_refs, refs = refs[:pieces], refs[pieces : pieces + 2 * chunks], refs[pieces + 2 * chunks :]
    user_refs, pack_refs, out_refs = refs[:chunks], refs[chunks : 2 * chunks], refs[2 * chunks :]
    held = halves(slab_of(held_refs))
    for i in range(chunks):
        out_ref, high_ref, low_ref, weights_ref, targets_ref = out_refs[5 * i : 5 * i + 5]
        users = out_ref.shape[0]
        move = product((errors_refs[2 * i][...], errors_refs[2 * i + 1][...]), held, TN)
        new = DECAY * user_refs[i][:users, :] - LEARN_RATE * move
        out_ref[...] = new
        high_ref[...], low_ref[...] = halves(new)
        weights_ref[...], targets_ref[...] = weigh(*listed(pack_refs[i], users, step + 1, obs), weights_ref.shape[0])


def last_kernel(pieces, chunks, *refs):
    held_refs, ready_refs, refs = refs[:pieces], refs[pieces : pieces + 4 * chunks], refs[pieces + 4 * chunks :]
    user_refs, out_ref, new_refs = refs[:chunks], refs[chunks], refs[chunks + 1 :]
    held = slab_of(held_refs)
    held_halves = halves(held)
    total = jnp.zeros(held.shape, jnp.float32)
    for i in range(chunks):
        high_ref, low_ref, weights_ref, targets_ref = ready_refs[4 * i : 4 * i + 4]
        user = high_ref[...], low_ref[...]
        errors = halves(weights_ref[...] * product(held_halves, user, NT) - targets_ref[...])
        total += product(errors, user, NN)
        new_refs[i][...] = DECAY * user_refs[i][...] - LEARN_RATE * product(errors, held_halves, TN)
    out_ref[...] = kept() * held - LEARN_RATE * total


def share_kernel(parts_ref, out_ref):
    out_ref[...] = parts_ref[FIRST ^ parity()] + parts_ref[SECOND ^ parity()]


def home_kernel(share_ref, own_ref, a_ref, b_ref, c_ref, out_ref, share_out_ref):
    share_out_ref[...] = share_ref[...]
    place = lax.axis_index("split") ^ parity()
    for ref, places in zip((own_ref, a_ref, b_ref, c_ref), ((FIRST, SECOND), *HELPERS)):

        @pl.when((place == places[0]) | (place == places[1]))
        def _(ref=ref):
            out_ref[...] = ref[...]


def local(user_factors, item_factors, obs_items, obs_conf):
    slab, rank = item_factors.shape
    users = user_factors.shape[0]
    _, steps, obs = obs_items.shape
    n = lax.axis_size("split")
    blocks = lax.axis_size("blk")
    share_rows = slab // n
    chunks = 1 + len(HELPERS)
    items = jnp.transpose(obs_items, (1, 2, 0))
    conf = jnp.transpose(obs_conf, (1, 2, 0))
    both = ("blk", "split")

    def at(b, k):
        return b * n + (k ^ (b & 1))

    def fetch(x, helpers):
        pairs = [(at(b, h), at(b, w)) for b in range(blocks) for h, w in zip(helpers, (FIRST, SECOND))]
        return lax.ppermute(x, both, pairs)

    def give(x, helpers):
        pairs = [(at(b, w), at(b, h)) for b in range(blocks) for h, w in zip(helpers, (FIRST, SECOND))]
        return lax.ppermute(x, both, pairs)

    def onward(x):
        same, cross = [], []
        for b in range(blocks):
            for w, v in ((FIRST, SECOND), (SECOND, FIRST)):
                source = at((b + 1) % blocks, w)
                same.append((source, at(b, w)))
                cross.append((source, at(b, v)))
        return [lax.ppermute(x, both, cross), lax.ppermute(x, both, same)]

    f32, bf16 = jnp.float32, jnp.bfloat16
    early = pl.CostEstimate(flops=1 << 36, bytes_accessed=1 << 20, transcendentals=0)
    hbm = pl.BlockSpec(memory_space=pltpu.HBM)
    rows = users + steps * obs
    part, pack = call(
        first_kernel,
        [((slab, rank), f32), ((rows, rank), f32)],
        "first",
        in_specs=[hbm] * 4,
        scratch_shapes=[pltpu.VMEM(user_factors.shape, f32), pltpu.VMEM(item_factors.shape, f32)]
        + [pltpu.VMEM(items.shape, jnp.int32)] * 2
        + [pltpu.SemaphoreType.DMA((4,))],
    )(*[pltpu.with_memory_space_constraint(x, pltpu.HBM) for x in (user_factors, item_factors, items, conf)])
    arrived = [part] + [fetch(part, helpers) for helpers in HELPERS]
    packs = [pack] + [fetch(pack, helpers) for helpers in HELPERS]
    (out,) = call(sum_kernel, [((slab, rank), f32)], "sum", cost_estimate=early)(*arrived)
    held = onward(out)
    factors, half, square = ((users, rank), f32), ((users, rank), bf16), ((slab, users), f32)
    pieces = len(held)
    ready = [half, half, square, square]
    kernel = functools.partial(prepare_kernel, 1, obs, chunks)
    ahead = call(kernel, ready * chunks, "prepare")(*packs)
    user = packs
    for step in range(1, steps - 1):
        kernel = functools.partial(group_kernel, pieces, chunks)
        outs = [((slab, rank), f32)] + [((slab, users), bf16)] * (2 * chunks)
        out, *errors = call(kernel, outs, "group")(*held, *ahead)
        sent = onward(out)
        kernel = functools.partial(users_kernel, step, obs, pieces, chunks)
        outs = call(kernel, [factors, *ready] * chunks, "users")(*held, *errors, *user, *packs)
        user = outs[::5]
        ahead = [x for i, x in enumerate(outs) if i % 5]
        held = sent
    kernel = functools.partial(last_kernel, pieces, chunks)
    out, *user = call(kernel, [((slab, rank), f32)] + [factors] * chunks, "last")(*held, *ahead, *user)
    parts = lax.all_to_all(out.reshape(n, share_rows, rank), "split", 0, 0)
    (share,) = call(share_kernel, [((share_rows, rank), f32)], "share", cost_estimate=early)(parts)
    share = lax.ppermute(share, "blk", [((b + 1) % blocks, b) for b in range(blocks)])
    home = [give(u, helpers) for u, helpers in zip(user[1:], HELPERS)]
    outs = [factors, ((share_rows, rank), f32)]
    user_out, share_out = call(home_kernel, outs, "home")(share, user[0], *home)
    return user_out, share_out


def solution(mesh):
    in_specs = (
        P(("blk", "split"), None),
        P("blk", None),
        P(("blk", "split"), None, None),
        P(("blk", "split"), None, None),
    )
    out_specs = (P(("blk", "split"), None), P(("blk", "split"), None))
    return jax.shard_map(local, mesh=mesh, in_specs=in_specs, out_specs=out_specs, check_vma=False)
```

```python
import functools

import jax
import jax.numpy as jnp
from jax import lax
from jax.experimental import pallas as pl
from jax.experimental.pallas import tpu as pltpu
from jax.sharding import PartitionSpec as P

LEARN_RATE = 0.0005
CONF_SCALE = 0.5
RIDGE_COEF = 0.01
DECAY = 1.0 - LEARN_RATE * RIDGE_COEF
PARAMS = pltpu.CompilerParams(vmem_limit_bytes=16 << 20)

NT = (((1,), (1,)), ((), ()))
NN = (((1,), (0,)), ((), ()))
TN = (((0,), (0,)), ((), ()))

FIRST, SECOND = 2, 7
HELPERS = ((0, 5), (4, 1), (3, 6))


def halves(x):
    high = x.astype(jnp.bfloat16)
    low = (x - high.astype(jnp.float32)).astype(jnp.bfloat16)
    return high, low


def product(a, b, dims):
    def one(p, q):
        return lax.dot_general(p, q, dims, preferred_element_type=jnp.float32)

    if dims == TN:
        return one(a[0], b[0]) + (one(a[0], b[1]) + one(a[1], b[0]))
    rows = a[0].shape[0]
    stacked = one(jnp.concatenate(a, axis=0), b[0])
    return stacked[:rows] + (stacked[rows:] + one(a[0], b[1]))


def weigh(items, conf, slab):
    rows = lax.broadcasted_iota(jnp.int32, (slab, items.shape[1]), 0)
    counts = jnp.zeros(rows.shape, jnp.float32)
    for k in range(items.shape[0]):
        counts += jnp.where(items[k : k + 1] == rows, conf[k : k + 1], 0.0)
    weights = 1.0 + CONF_SCALE * counts
    return weights, jnp.where(counts > 0.0, weights, 0.0)


def listed(ref, users, step, obs):
    at = users + step * obs
    return ref[at : at + obs, :users].astype(jnp.int32), ref[at : at + obs, users:]


def parity():
    return lax.axis_index("blk") & 1


def slab_of(refs):
    held = refs[0][...]
    for ref in refs[1:]:
        held += ref[...]
    return held


def call(kernel, outs, name, params=PARAMS, **kwargs):
    return pl.pallas_call(
        kernel,
        out_shape=[jax.ShapeDtypeStruct(shape, dtype) for shape, dtype in outs],
        compiler_params=params,
        name=name,
        **kwargs,
    )


def kept():
    return jnp.where((lax.axis_index("split") ^ parity()) == FIRST, DECAY, 0.0)


def first_kernel(user_hbm, held_hbm, items_hbm, conf_hbm, part, pack, user_ref, held_ref, items, conf, sems):
    users = user_ref.shape[0]
    slab = held_ref.shape[0]
    steps, obs, _ = items.shape
    pairs = ((items_hbm, items), (conf_hbm, conf), (held_hbm, held_ref), (user_hbm, user_ref))
    loads = [pltpu.make_async_copy(source, target, sems.at[i]) for i, (source, target) in enumerate(pairs)]
    for copy in loads:
        copy.start()
    loads[0].wait()
    loads[1].wait()
    for s in range(steps):
        at = users + s * obs
        pack[at : at + obs, :users] = items[s].astype(jnp.float32)
        pack[at : at + obs, users:] = conf[s].astype(jnp.float32)
    weights, targets = weigh(items[0], conf[0].astype(jnp.float32), slab)
    loads[2].wait()
    loads[3].wait()
    held = held_ref[...]
    held_halves = halves(held)
    user = halves(user_ref[...])
    errors = halves(weights * product(held_halves, user, NT) - targets)
    part[...] = kept() * held - LEARN_RATE * product(errors, user, NN)
    pack[:users, :] = DECAY * user_ref[...] - LEARN_RATE * product(errors, held_halves, TN)


def sum_kernel(*refs):
    refs[-1][...] = slab_of(refs[:-1])


def prepare_kernel(step, obs, chunks, *refs):
    pack_refs, out_refs = refs[:chunks], refs[chunks:]
    for i, pack_ref in enumerate(pack_refs):
        high_ref, low_ref, weights_ref, targets_ref = out_refs[4 * i : 4 * i + 4]
        users = high_ref.shape[0]
        high_ref[...], low_ref[...] = halves(pack_ref[:users, :])
        weights_ref[...], targets_ref[...] = weigh(*listed(pack_ref, users, step, obs), weights_ref.shape[0])


def group_kernel(pieces, chunks, *refs):
    held_refs, ready_refs, out_ref, errors_refs = refs[:pieces], refs[pieces : pieces + 4 * chunks], refs[pieces + 4 * chunks], refs[pieces + 4 * chunks + 1 :]
    held = slab_of(held_refs)
    held_halves = halves(held)
    total = jnp.zeros(held.shape, jnp.float32)
    for i in range(chunks):
        high_ref, low_ref, weights_ref, targets_ref = ready_refs[4 * i : 4 * i + 4]
        user = high_ref[...], low_ref[...]
        errors = halves(weights_ref[...] * product(held_halves, user, NT) - targets_ref[...])
        errors_refs[2 * i][...], errors_refs[2 * i + 1][...] = errors
        total += product(errors, user, NN)
    out_ref[...] = kept() * held - LEARN_RATE * total


def users_kernel(step, obs, pieces, chunks, *refs):
    held_refs, errors_refs, refs = refs[:pieces], refs[pieces : pieces + 2 * chunks], refs[pieces + 2 * chunks :]
    user_refs, pack_refs, out_refs = refs[:chunks], refs[chunks : 2 * chunks], refs[2 * chunks :]
    held = halves(slab_of(held_refs))
    for i in range(chunks):
        out_ref, high_ref, low_ref, weights_ref, targets_ref = out_refs[5 * i : 5 * i + 5]
        users = out_ref.shape[0]
        move = product((errors_refs[2 * i][...], errors_refs[2 * i + 1][...]), held, TN)
        new = DECAY * user_refs[i][:users, :] - LEARN_RATE * move
        out_ref[...] = new
        high_ref[...], low_ref[...] = halves(new)
        weights_ref[...], targets_ref[...] = weigh(*listed(pack_refs[i], users, step + 1, obs), weights_ref.shape[0])


def last_kernel(pieces, chunks, *refs):
    held_refs, ready_refs, refs = refs[:pieces], refs[pieces : pieces + 4 * chunks], refs[pieces + 4 * chunks :]
    user_refs, out_hbm, own_ref, new_hbm = refs[:chunks], refs[chunks], refs[chunks + 1], refs[chunks + 2 : 2 * chunks + 1]
    out, new, errors_ref, sems = refs[2 * chunks + 1 :]
    held = slab_of(held_refs)
    held_halves = halves(held)
    total = jnp.zeros(held.shape, jnp.float32)
    for i in range(chunks):
        high_ref, low_ref, weights_ref, targets_ref = ready_refs[4 * i : 4 * i + 4]
        user = high_ref[...], low_ref[...]
        errors = halves(weights_ref[...] * product(held_halves, user, NT) - targets_ref[...])
        errors_ref[2 * i], errors_ref[2 * i + 1] = errors
        total += product(errors, user, NN)
    out[...] = kept() * held - LEARN_RATE * total
    sends = [pltpu.make_async_copy(out, out_hbm, sems.at[0])]
    sends[0].start()
    for i in (*range(1, chunks), 0):
        move = product((errors_ref[2 * i], errors_ref[2 * i + 1]), held_halves, TN)
        moved = DECAY * user_refs[i][...] - LEARN_RATE * move
        if i == 0:
            own_ref[...] = moved
        else:
            new[i - 1] = moved
            sends.append(pltpu.make_async_copy(new.at[i - 1], new_hbm[i - 1], sems.at[i]))
            sends[-1].start()
    for send in sends:
        send.wait()


def share_kernel(parts_ref, out_ref):
    out_ref[...] = parts_ref[FIRST ^ parity()] + parts_ref[SECOND ^ parity()]


def home_kernel(share_ref, own_ref, a_ref, b_ref, c_ref, out_ref, share_out_ref):
    share_out_ref[...] = share_ref[...]
    place = lax.axis_index("split") ^ parity()
    for ref, places in zip((own_ref, a_ref, b_ref, c_ref), ((FIRST, SECOND), *HELPERS)):

        @pl.when((place == places[0]) | (place == places[1]))
        def _(ref=ref):
            out_ref[...] = ref[...]


def local(user_factors, item_factors, obs_items, obs_conf):
    slab, rank = item_factors.shape
    users = user_factors.shape[0]
    _, steps, obs = obs_items.shape
    n = lax.axis_size("split")
    blocks = lax.axis_size("blk")
    share_rows = slab // n
    chunks = 1 + len(HELPERS)
    items = jnp.transpose(obs_items, (1, 2, 0))
    conf = jnp.transpose(obs_conf, (1, 2, 0))
    both = ("blk", "split")

    def at(b, k):
        return b * n + (k ^ (b & 1))

    def fetch(x, helpers):
        pairs = [(at(b, h), at(b, w)) for b in range(blocks) for h, w in zip(helpers, (FIRST, SECOND))]
        return lax.ppermute(x, both, pairs)

    def give(x, helpers):
        pairs = [(at(b, w), at(b, h)) for b in range(blocks) for h, w in zip(helpers, (FIRST, SECOND))]
        return lax.ppermute(x, both, pairs)

    def onward(x):
        same, cross = [], []
        for b in range(blocks):
            for w, v in ((FIRST, SECOND), (SECOND, FIRST)):
                source = at((b + 1) % blocks, w)
                same.append((source, at(b, w)))
                cross.append((source, at(b, v)))
        return [lax.ppermute(x, both, cross), lax.ppermute(x, both, same)]

    f32, bf16 = jnp.float32, jnp.bfloat16
    early = pl.CostEstimate(flops=1 << 36, bytes_accessed=1 << 20, transcendentals=0)
    hbm = pl.BlockSpec(memory_space=pltpu.HBM)
    rows = users + steps * obs
    part, pack = call(
        first_kernel,
        [((slab, rank), f32), ((rows, rank), f32)],
        "first",
        in_specs=[hbm] * 4,
        scratch_shapes=[pltpu.VMEM(user_factors.shape, f32), pltpu.VMEM(item_factors.shape, f32)]
        + [pltpu.VMEM(items.shape, jnp.int32)] * 2
        + [pltpu.SemaphoreType.DMA((4,))],
    )(*[pltpu.with_memory_space_constraint(x, pltpu.HBM) for x in (user_factors, item_factors, items, conf)])
    arrived = [part] + [fetch(part, helpers) for helpers in HELPERS]
    packs = [pack] + [fetch(pack, helpers) for helpers in HELPERS]
    (out,) = call(sum_kernel, [((slab, rank), f32)], "sum", cost_estimate=early)(*arrived)
    held = onward(out)
    factors, half, square = ((users, rank), f32), ((users, rank), bf16), ((slab, users), f32)
    pieces = len(held)
    ready = [half, half, square, square]
    kernel = functools.partial(prepare_kernel, 1, obs, chunks)
    ahead = call(kernel, ready * chunks, "prepare")(*packs)
    user = packs
    for step in range(1, steps - 1):
        kernel = functools.partial(group_kernel, pieces, chunks)
        outs = [((slab, rank), f32)] + [((slab, users), bf16)] * (2 * chunks)
        out, *errors = call(kernel, outs, "group")(*held, *ahead)
        sent = onward(out)
        kernel = functools.partial(users_kernel, step, obs, pieces, chunks)
        outs = call(kernel, [factors, *ready] * chunks, "users")(*held, *errors, *user, *packs)
        user = outs[::5]
        ahead = [x for i, x in enumerate(outs) if i % 5]
        held = sent
    kernel = functools.partial(last_kernel, pieces, chunks)
    vmem = pl.BlockSpec(memory_space=pltpu.VMEM)
    out, *user = call(
        kernel,
        [((slab, rank), f32)] + [factors] * chunks,
        "last",
        out_specs=[hbm, vmem] + [hbm] * (chunks - 1),
        scratch_shapes=[pltpu.VMEM((slab, rank), f32), pltpu.VMEM((chunks - 1, users, rank), f32)]
        + [pltpu.VMEM((2 * chunks, slab, users), bf16), pltpu.SemaphoreType.DMA((chunks,))],
    )(*held, *ahead, *user)
    parts = lax.all_to_all(out.reshape(n, share_rows, rank), "split", 0, 0)
    (share,) = call(share_kernel, [((share_rows, rank), f32)], "share", cost_estimate=early)(parts)
    share = lax.ppermute(share, "blk", [((b + 1) % blocks, b) for b in range(blocks)])
    home = [give(u, helpers) for u, helpers in zip(user[1:], HELPERS)]
    outs = [factors, ((share_rows, rank), f32)]
    user_out, share_out = call(home_kernel, outs, "home")(share, user[0], *home)
    return user_out, share_out


def solution(mesh):
    in_specs = (
        P(("blk", "split"), None),
        P("blk", None),
        P(("blk", "split"), None, None),
        P(("blk", "split"), None, None),
    )
    out_specs = (P(("blk", "split"), None), P(("blk", "split"), None))
    return jax.shard_map(local, mesh=mesh, in_specs=in_specs, out_specs=out_specs, check_vma=False)
```

```python
import functools

import jax
import jax.numpy as jnp
from jax import lax
from jax.experimental import pallas as pl
from jax.experimental.pallas import tpu as pltpu
from jax.sharding import PartitionSpec as P

LEARN_RATE = 0.0005
CONF_SCALE = 0.5
RIDGE_COEF = 0.01
DECAY = 1.0 - LEARN_RATE * RIDGE_COEF
PARAMS = pltpu.CompilerParams(vmem_limit_bytes=16 << 20)

NT = (((1,), (1,)), ((), ()))
NN = (((1,), (0,)), ((), ()))
TN = (((0,), (0,)), ((), ()))

FIRST, SECOND = 2, 7
HELPERS = ((0, 5), (4, 1), (3, 6))


def halves(x):
    high = x.astype(jnp.bfloat16)
    low = (x - high.astype(jnp.float32)).astype(jnp.bfloat16)
    return high, low


def product(a, b, dims):
    def one(p, q):
        return lax.dot_general(p, q, dims, preferred_element_type=jnp.float32)

    if dims == TN:
        return one(a[0], b[0]) + (one(a[0], b[1]) + one(a[1], b[0]))
    rows = a[0].shape[0]
    stacked = one(jnp.concatenate(a, axis=0), b[0])
    return stacked[:rows] + (stacked[rows:] + one(a[0], b[1]))


def weigh(items, conf, slab):
    rows = lax.broadcasted_iota(jnp.int32, (slab, items.shape[1]), 0)
    counts = jnp.zeros(rows.shape, jnp.float32)
    for k in range(items.shape[0]):
        counts += jnp.where(items[k : k + 1] == rows, conf[k : k + 1], 0.0)
    weights = 1.0 + CONF_SCALE * counts
    return weights, jnp.where(counts > 0.0, weights, 0.0)


def listed(ref, users, step, obs):
    at = users + step * obs
    return ref[at : at + obs, :users].astype(jnp.int32), ref[at : at + obs, users:]


def parity():
    return lax.axis_index("blk") & 1


def slab_of(refs):
    held = refs[0][...]
    for ref in refs[1:]:
        held += ref[...]
    return held


def call(kernel, outs, name, params=PARAMS, **kwargs):
    return pl.pallas_call(
        kernel,
        out_shape=[jax.ShapeDtypeStruct(shape, dtype) for shape, dtype in outs],
        compiler_params=params,
        name=name,
        **kwargs,
    )


def kept():
    return jnp.where((lax.axis_index("split") ^ parity()) == FIRST, DECAY, 0.0)


def first_kernel(user_hbm, held_hbm, items_hbm, conf_hbm, part, errors_ref, held_ref, raw, items, conf, sems):
    slab, _ = held_ref.shape
    steps, obs, users = items.shape
    pairs = ((items_hbm, items), (conf_hbm, conf), (held_hbm, held_ref), (user_hbm, raw.at[pl.ds(0, users), :]))
    loads = [pltpu.make_async_copy(source, target, sems.at[i]) for i, (source, target) in enumerate(pairs)]
    for copy in loads:
        copy.start()
    loads[0].wait()
    loads[1].wait()
    for s in range(steps):
        at = users + s * obs
        raw[at : at + obs, :users] = items[s].astype(jnp.float32)
        raw[at : at + obs, users:] = conf[s].astype(jnp.float32)
    weights, targets = weigh(items[0], conf[0].astype(jnp.float32), slab)
    loads[2].wait()
    loads[3].wait()
    held = held_ref[...]
    user = halves(raw[:users, :])
    errors = halves(weights * product(halves(held), user, NT) - targets)
    errors_ref[0], errors_ref[1] = errors
    part[...] = kept() * held - LEARN_RATE * product(errors, user, NN)


def pack_kernel(raw, held_ref, errors_ref, pack):
    users = errors_ref.shape[2]
    move = product((errors_ref[0], errors_ref[1]), halves(held_ref[...]), TN)
    pack[:users, :] = DECAY * raw[:users, :] - LEARN_RATE * move
    pack[users:, :] = raw[users:, :]


def sum_kernel(*refs):
    refs[-1][...] = slab_of(refs[:-1])


def prepare_kernel(step, obs, chunks, *refs):
    pack_refs, out_refs = refs[:chunks], refs[chunks:]
    for i, pack_ref in enumerate(pack_refs):
        high_ref, low_ref, weights_ref, targets_ref = out_refs[4 * i : 4 * i + 4]
        users = high_ref.shape[0]
        high_ref[...], low_ref[...] = halves(pack_ref[:users, :])
        weights_ref[...], targets_ref[...] = weigh(*listed(pack_ref, users, step, obs), weights_ref.shape[0])


def group_kernel(pieces, chunks, *refs):
    held_refs, ready_refs, out_ref, errors_refs = refs[:pieces], refs[pieces : pieces + 4 * chunks], refs[pieces + 4 * chunks], refs[pieces + 4 * chunks + 1 :]
    held = slab_of(held_refs)
    held_halves = halves(held)
    total = jnp.zeros(held.shape, jnp.float32)
    for i in range(chunks):
        high_ref, low_ref, weights_ref, targets_ref = ready_refs[4 * i : 4 * i + 4]
        user = high_ref[...], low_ref[...]
        errors = halves(weights_ref[...] * product(held_halves, user, NT) - targets_ref[...])
        errors_refs[2 * i][...], errors_refs[2 * i + 1][...] = errors
        total += product(errors, user, NN)
    out_ref[...] = kept() * held - LEARN_RATE * total


def users_kernel(step, obs, pieces, chunks, *refs):
    held_refs, errors_refs, refs = refs[:pieces], refs[pieces : pieces + 2 * chunks], refs[pieces + 2 * chunks :]
    user_refs, pack_refs, out_refs = refs[:chunks], refs[chunks : 2 * chunks], refs[2 * chunks :]
    held = halves(slab_of(held_refs))
    for i in range(chunks):
        out_ref, high_ref, low_ref, weights_ref, targets_ref = out_refs[5 * i : 5 * i + 5]
        users = out_ref.shape[0]
        move = product((errors_refs[2 * i][...], errors_refs[2 * i + 1][...]), held, TN)
        new = DECAY * user_refs[i][:users, :] - LEARN_RATE * move
        out_ref[...] = new
        high_ref[...], low_ref[...] = halves(new)
        weights_ref[...], targets_ref[...] = weigh(*listed(pack_refs[i], users, step + 1, obs), weights_ref.shape[0])


def last_kernel(pieces, chunks, *refs):
    held_refs, ready_refs, refs = refs[:pieces], refs[pieces : pieces + 4 * chunks], refs[pieces + 4 * chunks :]
    user_refs, out_hbm, own_ref, new_hbm = refs[:chunks], refs[chunks], refs[chunks + 1], refs[chunks + 2 : 2 * chunks + 1]
    out, new, errors_ref, sems = refs[2 * chunks + 1 :]
    held = slab_of(held_refs)
    held_halves = halves(held)
    total = jnp.zeros(held.shape, jnp.float32)
    for i in range(chunks):
        high_ref, low_ref, weights_ref, targets_ref = ready_refs[4 * i : 4 * i + 4]
        user = high_ref[...], low_ref[...]
        errors = halves(weights_ref[...] * product(held_halves, user, NT) - targets_ref[...])
        errors_ref[2 * i], errors_ref[2 * i + 1] = errors
        total += product(errors, user, NN)
    out[...] = kept() * held - LEARN_RATE * total
    sends = [pltpu.make_async_copy(out, out_hbm, sems.at[0])]
    sends[0].start()
    for i in (*range(1, chunks), 0):
        move = product((errors_ref[2 * i], errors_ref[2 * i + 1]), held_halves, TN)
        moved = DECAY * user_refs[i][...] - LEARN_RATE * move
        if i == 0:
            own_ref[...] = moved
        else:
            new[i - 1] = moved
            sends.append(pltpu.make_async_copy(new.at[i - 1], new_hbm[i - 1], sems.at[i]))
            sends[-1].start()
    for send in sends:
        send.wait()


def share_kernel(parts_ref, out_ref):
    out_ref[...] = parts_ref[FIRST ^ parity()] + parts_ref[SECOND ^ parity()]


def home_kernel(share_ref, own_ref, a_ref, b_ref, c_ref, out_ref, share_out_ref):
    share_out_ref[...] = share_ref[...]
    place = lax.axis_index("split") ^ parity()
    for ref, places in zip((own_ref, a_ref, b_ref, c_ref), ((FIRST, SECOND), *HELPERS)):

        @pl.when((place == places[0]) | (place == places[1]))
        def _(ref=ref):
            out_ref[...] = ref[...]


def local(user_factors, item_factors, obs_items, obs_conf):
    slab, rank = item_factors.shape
    users = user_factors.shape[0]
    _, steps, obs = obs_items.shape
    n = lax.axis_size("split")
    blocks = lax.axis_size("blk")
    share_rows = slab // n
    chunks = 1 + len(HELPERS)
    items = jnp.transpose(obs_items, (1, 2, 0))
    conf = jnp.transpose(obs_conf, (1, 2, 0))
    both = ("blk", "split")

    def at(b, k):
        return b * n + (k ^ (b & 1))

    def fetch(x, helpers):
        pairs = [(at(b, h), at(b, w)) for b in range(blocks) for h, w in zip(helpers, (FIRST, SECOND))]
        return lax.ppermute(x, both, pairs)

    def give(x, helpers):
        pairs = [(at(b, w), at(b, h)) for b in range(blocks) for h, w in zip(helpers, (FIRST, SECOND))]
        return lax.ppermute(x, both, pairs)

    def onward(x):
        same, cross = [], []
        for b in range(blocks):
            for w, v in ((FIRST, SECOND), (SECOND, FIRST)):
                source = at((b + 1) % blocks, w)
                same.append((source, at(b, w)))
                cross.append((source, at(b, v)))
        return [lax.ppermute(x, both, cross), lax.ppermute(x, both, same)]

    f32, bf16 = jnp.float32, jnp.bfloat16
    early = pl.CostEstimate(flops=1 << 36, bytes_accessed=1 << 20, transcendentals=0)
    hbm = pl.BlockSpec(memory_space=pltpu.HBM)
    rows = users + steps * obs
    part, first_errors, slab_copy, raw = call(
        first_kernel,
        [((slab, rank), f32), ((2, slab, users), bf16), ((slab, rank), f32), ((rows, rank), f32)],
        "first",
        in_specs=[hbm] * 4,
        scratch_shapes=[pltpu.VMEM(items.shape, jnp.int32)] * 2 + [pltpu.SemaphoreType.DMA((4,))],
    )(*[pltpu.with_memory_space_constraint(x, pltpu.HBM) for x in (user_factors, item_factors, items, conf)])
    (pack,) = call(pack_kernel, [((rows, rank), f32)], "pack")(raw, slab_copy, first_errors)
    arrived = [part] + [fetch(part, helpers) for helpers in HELPERS]
    packs = [pack] + [fetch(pack, helpers) for helpers in HELPERS]
    (out,) = call(sum_kernel, [((slab, rank), f32)], "sum", cost_estimate=early)(*arrived)
    held = onward(out)
    factors, half, square = ((users, rank), f32), ((users, rank), bf16), ((slab, users), f32)
    pieces = len(held)
    ready = [half, half, square, square]
    kernel = functools.partial(prepare_kernel, 1, obs, chunks)
    ahead = call(kernel, ready * chunks, "prepare")(*packs)
    user = packs
    for step in range(1, steps - 1):
        kernel = functools.partial(group_kernel, pieces, chunks)
        outs = [((slab, rank), f32)] + [((slab, users), bf16)] * (2 * chunks)
        out, *errors = call(kernel, outs, "group")(*held, *ahead)
        sent = onward(out)
        kernel = functools.partial(users_kernel, step, obs, pieces, chunks)
        outs = call(kernel, [factors, *ready] * chunks, "users")(*held, *errors, *user, *packs)
        user = outs[::5]
        ahead = [x for i, x in enumerate(outs) if i % 5]
        held = sent
    kernel = functools.partial(last_kernel, pieces, chunks)
    vmem = pl.BlockSpec(memory_space=pltpu.VMEM)
    out, *user = call(
        kernel,
        [((slab, rank), f32)] + [factors] * chunks,
        "last",
        out_specs=[hbm, vmem] + [hbm] * (chunks - 1),
        scratch_shapes=[pltpu.VMEM((slab, rank), f32), pltpu.VMEM((chunks - 1, users, rank), f32)]
        + [pltpu.VMEM((2 * chunks, slab, users), bf16), pltpu.SemaphoreType.DMA((chunks,))],
    )(*held, *ahead, *user)
    parts = lax.all_to_all(out.reshape(n, share_rows, rank), "split", 0, 0)
    (share,) = call(share_kernel, [((share_rows, rank), f32)], "share", cost_estimate=early)(parts)
    share = lax.ppermute(share, "blk", [((b + 1) % blocks, b) for b in range(blocks)])
    home = [give(u, helpers) for u, helpers in zip(user[1:], HELPERS)]
    outs = [factors, ((share_rows, rank), f32)]
    user_out, share_out = call(home_kernel, outs, "home")(share, user[0], *home)
    return user_out, share_out


def solution(mesh):
    in_specs = (
        P(("blk", "split"), None),
        P("blk", None),
        P(("blk", "split"), None, None),
        P(("blk", "split"), None, None),
    )
    out_specs = (P(("blk", "split"), None), P(("blk", "split"), None))
    return jax.shard_map(local, mesh=mesh, in_specs=in_specs, out_specs=out_specs, check_vma=False)
```

```python
import functools

import jax
import jax.numpy as jnp
from jax import lax
from jax.experimental import pallas as pl
from jax.experimental.pallas import tpu as pltpu
from jax.sharding import PartitionSpec as P

LEARN_RATE = 0.0005
CONF_SCALE = 0.5
RIDGE_COEF = 0.01
DECAY = 1.0 - LEARN_RATE * RIDGE_COEF
PARAMS = pltpu.CompilerParams(vmem_limit_bytes=16 << 20)

NT = (((1,), (1,)), ((), ()))
NN = (((1,), (0,)), ((), ()))
TN = (((0,), (0,)), ((), ()))

FIRST, SECOND = 2, 7
HELPERS = ((0, 5), (4, 1), (3, 6))


def halves(x):
    high = x.astype(jnp.bfloat16)
    low = (x - high.astype(jnp.float32)).astype(jnp.bfloat16)
    return high, low


def product(a, b, dims):
    def one(p, q):
        return lax.dot_general(p, q, dims, preferred_element_type=jnp.float32)

    if dims == TN:
        return one(a[0], b[0]) + (one(a[0], b[1]) + one(a[1], b[0]))
    rows = a[0].shape[0]
    stacked = one(jnp.concatenate(a, axis=0), b[0])
    return stacked[:rows] + (stacked[rows:] + one(a[0], b[1]))


def weigh(items, conf, slab):
    rows = lax.broadcasted_iota(jnp.int32, (slab, items.shape[1]), 0)
    counts = jnp.zeros(rows.shape, jnp.float32)
    for k in range(items.shape[0]):
        counts += jnp.where(items[k : k + 1] == rows, conf[k : k + 1], 0.0)
    weights = 1.0 + CONF_SCALE * counts
    return weights, jnp.where(counts > 0.0, weights, 0.0)


def listed(ref, users, step, obs):
    at = users + step * obs
    return ref[at : at + obs, :users].astype(jnp.int32), ref[at : at + obs, users:]


def parity():
    return lax.axis_index("blk") & 1


def slab_of(refs):
    held = refs[0][...]
    for ref in refs[1:]:
        held += ref[...]
    return held


def call(kernel, outs, name, params=PARAMS, **kwargs):
    return pl.pallas_call(
        kernel,
        out_shape=[jax.ShapeDtypeStruct(shape, dtype) for shape, dtype in outs],
        compiler_params=params,
        name=name,
        **kwargs,
    )


def kept():
    return jnp.where((lax.axis_index("split") ^ parity()) == FIRST, DECAY, 0.0)


def first_kernel(user_hbm, held_hbm, items_hbm, conf_hbm, part, errors_ref, held_ref, raw, items, conf, sems):
    slab, _ = held_ref.shape
    steps, obs, users = items.shape
    half = held_ref.shape[1] // 2
    columns = [pl.ds(0, half), pl.ds(half, half)]
    pairs = [(items_hbm, items), (conf_hbm, conf), (held_hbm, held_ref)]
    pairs += [(user_hbm.at[:, c], raw.at[pl.ds(0, users), c]) for c in columns]
    loads = [pltpu.make_async_copy(source, target, sems.at[i]) for i, (source, target) in enumerate(pairs)]
    for copy in loads:
        copy.start()
    loads[0].wait()
    loads[1].wait()
    for s in range(steps):
        at = users + s * obs
        raw[at : at + obs, :users] = items[s].astype(jnp.float32)
        raw[at : at + obs, users:] = conf[s].astype(jnp.float32)
    weights, targets = weigh(items[0], conf[0].astype(jnp.float32), slab)
    loads[2].wait()
    scores, user = jnp.zeros((slab, users), jnp.float32), []
    for c, load in zip(columns, loads[3:]):
        load.wait()
        user.append(halves(raw[:users, c]))
        scores += product(halves(held_ref[:, c]), user[-1], NT)
    errors = halves(weights * scores - targets)
    errors_ref[0], errors_ref[1] = errors
    for c, piece in zip(columns, user):
        part[:, c] = kept() * held_ref[:, c] - LEARN_RATE * product(errors, piece, NN)


def pack_kernel(raw, held_ref, errors_ref, pack):
    users = errors_ref.shape[2]
    move = product((errors_ref[0], errors_ref[1]), halves(held_ref[...]), TN)
    pack[:users, :] = DECAY * raw[:users, :] - LEARN_RATE * move
    pack[users:, :] = raw[users:, :]


def sum_kernel(*refs):
    refs[-1][...] = slab_of(refs[:-1])


def prepare_kernel(step, obs, chunks, *refs):
    pack_refs, out_refs = refs[:chunks], refs[chunks:]
    for i, pack_ref in enumerate(pack_refs):
        high_ref, low_ref, weights_ref, targets_ref = out_refs[4 * i : 4 * i + 4]
        users = high_ref.shape[0]
        high_ref[...], low_ref[...] = halves(pack_ref[:users, :])
        weights_ref[...], targets_ref[...] = weigh(*listed(pack_ref, users, step, obs), weights_ref.shape[0])


def group_kernel(pieces, chunks, *refs):
    held_refs, ready_refs, out_ref, errors_refs = refs[:pieces], refs[pieces : pieces + 4 * chunks], refs[pieces + 4 * chunks], refs[pieces + 4 * chunks + 1 :]
    held = slab_of(held_refs)
    held_halves = halves(held)
    total = jnp.zeros(held.shape, jnp.float32)
    for i in range(chunks):
        high_ref, low_ref, weights_ref, targets_ref = ready_refs[4 * i : 4 * i + 4]
        user = high_ref[...], low_ref[...]
        errors = halves(weights_ref[...] * product(held_halves, user, NT) - targets_ref[...])
        errors_refs[2 * i][...], errors_refs[2 * i + 1][...] = errors
        total += product(errors, user, NN)
    out_ref[...] = kept() * held - LEARN_RATE * total


def users_kernel(step, obs, pieces, chunks, *refs):
    held_refs, errors_refs, refs = refs[:pieces], refs[pieces : pieces + 2 * chunks], refs[pieces + 2 * chunks :]
    user_refs, pack_refs, out_refs = refs[:chunks], refs[chunks : 2 * chunks], refs[2 * chunks :]
    held = halves(slab_of(held_refs))
    for i in range(chunks):
        out_ref, high_ref, low_ref, weights_ref, targets_ref = out_refs[5 * i : 5 * i + 5]
        users = out_ref.shape[0]
        move = product((errors_refs[2 * i][...], errors_refs[2 * i + 1][...]), held, TN)
        new = DECAY * user_refs[i][:users, :] - LEARN_RATE * move
        out_ref[...] = new
        high_ref[...], low_ref[...] = halves(new)
        weights_ref[...], targets_ref[...] = weigh(*listed(pack_refs[i], users, step + 1, obs), weights_ref.shape[0])


def last_kernel(pieces, chunks, *refs):
    held_refs, ready_refs, refs = refs[:pieces], refs[pieces : pieces + 4 * chunks], refs[pieces + 4 * chunks :]
    user_refs, out_hbm, own_ref, new_hbm = refs[:chunks], refs[chunks], refs[chunks + 1], refs[chunks + 2 : 2 * chunks + 1]
    out, new, errors_ref, sems = refs[2 * chunks + 1 :]
    held = slab_of(held_refs)
    held_halves = halves(held)
    total = jnp.zeros(held.shape, jnp.float32)
    for i in range(chunks):
        high_ref, low_ref, weights_ref, targets_ref = ready_refs[4 * i : 4 * i + 4]
        user = high_ref[...], low_ref[...]
        errors = halves(weights_ref[...] * product(held_halves, user, NT) - targets_ref[...])
        errors_ref[2 * i], errors_ref[2 * i + 1] = errors
        total += product(errors, user, NN)
    out[...] = kept() * held - LEARN_RATE * total
    sends = [pltpu.make_async_copy(out, out_hbm, sems.at[0])]
    sends[0].start()
    for i in (*range(1, chunks), 0):
        move = product((errors_ref[2 * i], errors_ref[2 * i + 1]), held_halves, TN)
        moved = DECAY * user_refs[i][...] - LEARN_RATE * move
        if i == 0:
            own_ref[...] = moved
        else:
            new[i - 1] = moved
            sends.append(pltpu.make_async_copy(new.at[i - 1], new_hbm[i - 1], sems.at[i]))
            sends[-1].start()
    for send in sends:
        send.wait()


def share_kernel(parts_ref, out_ref):
    out_ref[...] = parts_ref[FIRST ^ parity()] + parts_ref[SECOND ^ parity()]


def home_kernel(share_ref, own_ref, a_ref, b_ref, c_ref, out_ref, share_out_ref):
    share_out_ref[...] = share_ref[...]
    place = lax.axis_index("split") ^ parity()
    for ref, places in zip((own_ref, a_ref, b_ref, c_ref), ((FIRST, SECOND), *HELPERS)):

        @pl.when((place == places[0]) | (place == places[1]))
        def _(ref=ref):
            out_ref[...] = ref[...]


def local(user_factors, item_factors, obs_items, obs_conf):
    slab, rank = item_factors.shape
    users = user_factors.shape[0]
    _, steps, obs = obs_items.shape
    n = lax.axis_size("split")
    blocks = lax.axis_size("blk")
    share_rows = slab // n
    chunks = 1 + len(HELPERS)
    items = jnp.transpose(obs_items, (1, 2, 0))
    conf = jnp.transpose(obs_conf, (1, 2, 0))
    both = ("blk", "split")

    def at(b, k):
        return b * n + (k ^ (b & 1))

    def fetch(x, helpers):
        pairs = [(at(b, h), at(b, w)) for b in range(blocks) for h, w in zip(helpers, (FIRST, SECOND))]
        return lax.ppermute(x, both, pairs)

    def give(x, helpers):
        pairs = [(at(b, w), at(b, h)) for b in range(blocks) for h, w in zip(helpers, (FIRST, SECOND))]
        return lax.ppermute(x, both, pairs)

    def onward(x):
        same, cross = [], []
        for b in range(blocks):
            for w, v in ((FIRST, SECOND), (SECOND, FIRST)):
                source = at((b + 1) % blocks, w)
                same.append((source, at(b, w)))
                cross.append((source, at(b, v)))
        return [lax.ppermute(x, both, cross), lax.ppermute(x, both, same)]

    f32, bf16 = jnp.float32, jnp.bfloat16
    early = pl.CostEstimate(flops=1 << 36, bytes_accessed=1 << 20, transcendentals=0)
    hbm = pl.BlockSpec(memory_space=pltpu.HBM)
    rows = users + steps * obs
    part, first_errors, slab_copy, raw = call(
        first_kernel,
        [((slab, rank), f32), ((2, slab, users), bf16), ((slab, rank), f32), ((rows, rank), f32)],
        "first",
        in_specs=[hbm] * 4,
        scratch_shapes=[pltpu.VMEM(items.shape, jnp.int32)] * 2 + [pltpu.SemaphoreType.DMA((5,))],
    )(*[pltpu.with_memory_space_constraint(x, pltpu.HBM) for x in (user_factors, item_factors, items, conf)])
    (pack,) = call(pack_kernel, [((rows, rank), f32)], "pack")(raw, slab_copy, first_errors)
    arrived = [part] + [fetch(part, helpers) for helpers in HELPERS]
    packs = [pack] + [fetch(pack, helpers) for helpers in HELPERS]
    (out,) = call(sum_kernel, [((slab, rank), f32)], "sum", cost_estimate=early)(*arrived)
    held = onward(out)
    factors, half, square = ((users, rank), f32), ((users, rank), bf16), ((slab, users), f32)
    pieces = len(held)
    ready = [half, half, square, square]
    kernel = functools.partial(prepare_kernel, 1, obs, chunks)
    ahead = call(kernel, ready * chunks, "prepare")(*packs)
    user = packs
    for step in range(1, steps - 1):
        kernel = functools.partial(group_kernel, pieces, chunks)
        outs = [((slab, rank), f32)] + [((slab, users), bf16)] * (2 * chunks)
        out, *errors = call(kernel, outs, "group")(*held, *ahead)
        sent = onward(out)
        kernel = functools.partial(users_kernel, step, obs, pieces, chunks)
        outs = call(kernel, [factors, *ready] * chunks, "users")(*held, *errors, *user, *packs)
        user = outs[::5]
        ahead = [x for i, x in enumerate(outs) if i % 5]
        held = sent
    kernel = functools.partial(last_kernel, pieces, chunks)
    vmem = pl.BlockSpec(memory_space=pltpu.VMEM)
    out, *user = call(
        kernel,
        [((slab, rank), f32)] + [factors] * chunks,
        "last",
        out_specs=[hbm, vmem] + [hbm] * (chunks - 1),
        scratch_shapes=[pltpu.VMEM((slab, rank), f32), pltpu.VMEM((chunks - 1, users, rank), f32)]
        + [pltpu.VMEM((2 * chunks, slab, users), bf16), pltpu.SemaphoreType.DMA((chunks,))],
    )(*held, *ahead, *user)
    parts = lax.all_to_all(out.reshape(n, share_rows, rank), "split", 0, 0)
    (share,) = call(share_kernel, [((share_rows, rank), f32)], "share", cost_estimate=early)(parts)
    share = lax.ppermute(share, "blk", [((b + 1) % blocks, b) for b in range(blocks)])
    home = [give(u, helpers) for u, helpers in zip(user[1:], HELPERS)]
    outs = [factors, ((share_rows, rank), f32)]
    user_out, share_out = call(home_kernel, outs, "home")(share, user[0], *home)
    return user_out, share_out


def solution(mesh):
    in_specs = (
        P(("blk", "split"), None),
        P("blk", None),
        P(("blk", "split"), None, None),
        P(("blk", "split"), None, None),
    )
    out_specs = (P(("blk", "split"), None), P(("blk", "split"), None))
    return jax.shard_map(local, mesh=mesh, in_specs=in_specs, out_specs=out_specs, check_vma=False)
```
